128 devices in a mesh: blk: 16 (over y_hi, x, core), expert: 8 (over y_lo, z).
Axes of the slice: x: 4, y: 4 (y_hi: 2, y_lo: 2; y = y_hi * 2 + y_lo), z: 4, core: 2. Of those that a mesh axis runs over, the one named last changes fastest.
Arguments:
- q_new: bfloat16 [1024, 8, 2304], P('blk', 'expert'), may hold values from -6 to 6
- k_new: bfloat16 [1024, 8, 2304], P('blk', 'expert'), may hold values from -8 to 8
- v_new: bfloat16 [1024, 8, 2304], P('blk', 'expert'), may hold values from -6 to 6
- cache_k: bfloat16 [2048, 8, 2304], P('blk', 'expert'), may hold values from -8 to 8
- cache_v: bfloat16 [2048, 8, 2304], P('blk', 'expert'), may hold values from -6 to 6
- cache_len: int32 [8], P('expert'), may hold values from 1 to 2048, as said below
- residual: bfloat16 [1024, 8, 2304], P('blk', 'expert'), may hold values from -8 to 8
- w_out: bfloat16 [2304, 2304], replicated, may hold values from -0.125 to 0.125
- norm_gain: float32 [2304], replicated, may hold values from 0.5 to 1.5
- expert_ids: int32 [1024, 8, 2], P('blk'), may hold values from 0 to 7, all different within a row; in each aligned block of 512 rows (0 to 511, 512 to 1023, ..., all dimensions but the last counted through in order) at most 136 rows name the same one
- gate_weights: float32 [1024, 8, 2], P('blk'), may hold values from 0.1 to 0.9
- w_gate: bfloat16 [8, 5760, 2304], P('expert', 'blk'), may hold values from -0.125 to 0.125
- w_up: bfloat16 [8, 5760, 2304], P('expert', 'blk'), may hold values from -0.125 to 0.125
- w_down: bfloat16 [8, 5760, 2304], P('expert', 'blk'), may hold values from -0.078125 to 0.078125
Outputs:
- layer_out: bfloat16 [1024, 8, 2304], P('blk', 'expert')
The draws below stay inside these ranges and needn't reach their ends.
Inputs may be any that keep to these rules, and one draw needn't show every extreme that they name: `expert_ids`: each row names 2 different experts. In each aligned block of 512 rows (positions b * 64 to (b + 1) * 64 - 1 of all requests) no expert is named by more than 136 rows, and in every draw some expert is named by exactly 136 rows of some block. `cache_len`: in every draw some request's cache is full, 2048 rows.
All inputs are finite; a program needn't handle non-finite values.
Results may differ from the reference program's by a relative error of at most 0.014.
Values may be sent and summed in bfloat16 or wider, within the bound.
A program may use at most 192 MiB of HBM per device.

```python
import math
import jax
import jax.numpy as jnp
import numpy as np
from jax import lax

D = 2304
HEADS = 36
HEAD_DIM = 64
FF = 5760
TOP = 2
EXPERTS = 8
Q_DEV = 64
REQ = 8
NEW = 1024
CACHE = 2048
CAP = 136
N_BLK = 16


def scaled_keys(seed_key, salt, row_count):
    shape = (row_count, REQ, D)
    drawn_rows = jnp.clip(jax.random.normal(jax.random.fold_in(seed_key, salt), shape), -4.0, 4.0)
    row_scale = jnp.exp(jax.random.uniform(jax.random.fold_in(seed_key, salt + 1), (row_count, REQ, 1), minval=math.log(0.35), maxval=math.log(3.5)))
    return jnp.clip(drawn_rows * row_scale, -8.0, 8.0)


def draw_q_new(key, part):
    shape = (NEW, REQ, D)
    drawn_rows = jnp.clip(jax.random.normal(jax.random.fold_in(key, 11), shape), -6.0, 6.0)
    return drawn_rows.astype(jnp.bfloat16)


def draw_k_new(key, part):
    drawn_rows = scaled_keys(key, 21, NEW)
    return drawn_rows.astype(jnp.bfloat16)


def draw_cache_k(key, part):
    return scaled_keys(key, 31, CACHE).astype(jnp.bfloat16)


def draw_cache_len(key, part):
    lengths = jax.random.randint(jax.random.fold_in(key, 41), (REQ,), 1, CACHE + 1)
    full_one = jax.random.randint(jax.random.fold_in(key, 42), (), 0, REQ)
    return jnp.where(jnp.arange(REQ) == full_one, CACHE, lengths).astype(jnp.int32)


def draw_residual(key, part):
    shape = (NEW, REQ, D)
    column_scale = jnp.exp(jax.random.uniform(jax.random.fold_in(key, 52), (1, 1, D), minval=math.log(0.3), maxval=math.log(3.0)))
    row_scale = jnp.exp(jax.random.uniform(jax.random.fold_in(key, 51), (NEW, REQ, 1), minval=math.log(0.3), maxval=math.log(3.0)))
    mixed_rows = jax.random.normal(jax.random.fold_in(key, 54), shape)
    return jnp.clip(0.5 * mixed_rows * row_scale * column_scale, -8.0, 8.0).astype(jnp.bfloat16)


def block_levels(key, dims, shards, least, high):
    factor_of, own = 1.0, jax.random.fold_in(key, 6)
    for position, shards_of in shards:
        draws = jnp.exp(jax.random.uniform(jax.random.fold_in(own, position), (shards_of,), jnp.float32, least / len(shards), high / len(shards)))
        factor_of = factor_of * jnp.repeat(draws, dims[position] // shards_of).reshape([-1 if axis == position else 1 for axis in range(len(dims))])
    return factor_of


def assign_block(rng, own, number, rows, amount, top, reach, lean):
    order = jax.random.permutation(rng, amount)
    heavy_load, usual = portions_of(amount, rows * top, reach, lean, True), portions_of(amount, rows * top, reach, lean, False)
    places = jnp.arange(amount)

    def named(sizes, offset_by):
        used = int((sizes > 0).sum())
        fixed = max(1, used // 4)
        shifted = fixed + (places - fixed + offset_by * (used - fixed)) % max(1, amount - fixed)
        return jnp.zeros((amount,), jnp.int32).at[order[jnp.where(places < fixed, places, shifted)]].set(jnp.asarray(sizes, jnp.int32))

    sizes = jnp.where(number % 4 == 0, named(heavy_load, number // 4), named(usual, number - number // 4 - 1))
    mixed = jax.random.permutation(jax.random.fold_in(own, 3), amount)
    giver, sink = mixed[0:amount // 2 * 2:2], mixed[1:amount // 2 * 2:2]
    margin = jnp.minimum(sizes[giver] - 1, reach - sizes[sink]) // 2
    margin = jnp.where((giver == order[0]) | (sink == order[0]) | (sizes[sink] == 0), 0, jnp.maximum(margin, 0))
    shifted = jax.random.randint(jax.random.fold_in(own, 4), (amount // 2,), 0, 1 << 20) % (margin + 1)
    sizes = sizes.at[giver].add(-shifted).at[sink].add(shifted)
    items = jnp.searchsorted(jnp.cumsum(sizes), jnp.arange(rows * top), side="right").astype(jnp.int32)
    listing = items.reshape(top, rows).T
    listing = listing[jax.random.permutation(jax.random.fold_in(own, 1), rows)]
    offset_by = jax.random.randint(jax.random.fold_in(own, 2), (rows, 1), 0, top)
    return jnp.take_along_axis(listing, (jnp.arange(top)[None, :] + offset_by) % top, axis=1)


def portions_of(count, total, most, slope, full):
    portions = [(1 << 20) // math.isqrt(standing ** slope) + 1 for standing in range(1, count + 1)]
    largest = most if full else min(most, max(-(-total // count), total * portions[0] // sum(portions)))
    least = 1 if total - largest >= count - 1 else 0
    given, spare = [largest] + [least] * (count - 1), total - largest - least * (count - 1)
    while spare > 0:
        candidates = [i for i in range(1, count) if given[i] < largest] or [i for i in range(1, count) if given[i] < most]
        pool, remaining = sum([portions[i] for i in candidates]), spare
        for i in candidates:
            more = min(most - given[i], max(1, remaining * portions[i] // pool), spare)
            given[i] = given[i] + more
            spare = spare - more
    return np.array(given)


def centred(key, extent, deviation, reach, shards=(), kind=jnp.bfloat16):
    gain = block_levels(key, extent, shards, -0.22, 0.18) if shards else 1.0
    entries = jax.random.normal(key, extent, jnp.float32) * deviation * gain
    return jnp.minimum(jnp.maximum(entries, -reach), reach).astype(kind)


def setup_inputs(seed: int = 0) -> dict:
    arg_keys = jax.random.split(jax.random.key(seed), 15)
    q_new = draw_q_new(jax.random.fold_in(arg_keys[14], 71), 0)
    k_new = draw_k_new(jax.random.fold_in(arg_keys[14], 71), 0)
    v_new = centred(arg_keys[2], (NEW, REQ, D), 1.0, 6.0, ((0, 16), (1, 8)))
    cache_k = draw_cache_k(jax.random.fold_in(arg_keys[14], 71), 0)
    cache_v = centred(arg_keys[4], (CACHE, REQ, D), 1.0, 6.0, ((0, 16), (1, 8)))
    cache_len = draw_cache_len(jax.random.fold_in(arg_keys[14], 71), 0)
    residual = draw_residual(jax.random.fold_in(arg_keys[14], 71), 0)
    w_out = centred(arg_keys[7], (D, D), D ** -0.5, 0.125)
    norm_gain = jnp.clip(1.0 + 0.1 * jax.random.normal(arg_keys[8], (D,), jnp.float32), 0.5, 1.5)
    expert_ids_keys = jax.random.split(jax.random.fold_in(arg_keys[9], 1), NEW * REQ // (Q_DEV * REQ))
    expert_ids_turns = jax.random.permutation(jax.random.fold_in(arg_keys[9], 3), NEW * REQ // (Q_DEV * REQ))
    expert_ids = jax.vmap(lambda own, number: assign_block(jax.random.fold_in(arg_keys[9], 2), own, number, Q_DEV * REQ, EXPERTS, TOP, CAP, 0))(expert_ids_keys, expert_ids_turns).reshape((NEW, REQ, TOP))
    gate_weights = jnp.clip(0.1 + 0.79999997 * jax.random.uniform(arg_keys[10], (NEW, REQ, TOP), jnp.float32) ** block_levels(arg_keys[10], (NEW, REQ, TOP), ((0, 16),), -0.2, 0.2), 0.1, 0.9)
    w_gate = centred(arg_keys[11], (EXPERTS, FF, D), D ** -0.5, 0.125, ((0, 8), (1, 16)))
    w_up = centred(arg_keys[12], (EXPERTS, FF, D), D ** -0.5, 0.125, ((0, 8), (1, 16)))
    w_down = centred(arg_keys[13], (EXPERTS, FF, D), FF ** -0.5, 0.078125, ((0, 8), (1, 16)))
    return dict(q_new=q_new, k_new=k_new, v_new=v_new, cache_k=cache_k, cache_v=cache_v, cache_len=cache_len, residual=residual, w_out=w_out, norm_gain=norm_gain, expert_ids=expert_ids, gate_weights=gate_weights, w_gate=w_gate, w_up=w_up, w_down=w_down)


epsilon = 1e-05

def attend_request(request_data):
    queries, keys_cache, keys_fresh, values_cache, values_fresh, length = request_data
    key_rows = jnp.concatenate([keys_cache, keys_fresh], 0).reshape(CACHE + NEW, HEADS, HEAD_DIM).astype(jnp.float32)
    value_rows = jnp.concatenate([values_cache, values_fresh], 0).reshape(CACHE + NEW, HEADS, HEAD_DIM).astype(jnp.float32)
    query_heads = queries.reshape(NEW, HEADS, HEAD_DIM).astype(jnp.float32)
    scores = jnp.einsum('qhd,khd->hqk', query_heads, key_rows) * HEAD_DIM ** (-0.5)
    positions = jnp.arange(NEW)
    cache_ok = jnp.broadcast_to((jnp.arange(CACHE) < length)[None, :], (NEW, CACHE))
    new_ok = positions[None, :] <= positions[:, None]
    visible = jnp.concatenate([cache_ok, new_ok], 1)[None]
    row_max = lax.optimization_barrier(jnp.max(jnp.where(visible, scores, -jnp.inf), axis=2, keepdims=True))
    weights = jnp.where(visible, jnp.exp(scores - row_max), 0.0)
    row_total = lax.optimization_barrier(jnp.sum(weights, axis=2))
    rounded = lax.optimization_barrier(weights.astype(jnp.bfloat16)).astype(jnp.float32)
    mixed_heads = jnp.einsum('hqk,khd->hqd', rounded, value_rows) / row_total[:, :, None]
    return jnp.transpose(mixed_heads, (1, 0, 2)).reshape(NEW, D).astype(jnp.bfloat16)

def add_block(running, block_pair):
    part_sum = jnp.dot(block_pair[0], block_pair[1], preferred_element_type=jnp.float32)
    rounded_part = lax.optimization_barrier(part_sum.astype(jnp.bfloat16))
    return (running + rounded_part.astype(jnp.float32), None)

def reference(q_new, k_new, v_new, cache_k, cache_v, cache_len, residual, w_out, norm_gain, expert_ids, gate_weights, w_gate, w_up, w_down):
    attended = lax.map(attend_request, (jnp.moveaxis(q_new, 1, 0), jnp.moveaxis(cache_k, 1, 0), jnp.moveaxis(k_new, 1, 0), jnp.moveaxis(cache_v, 1, 0), jnp.moveaxis(v_new, 1, 0), cache_len))
    attended = jnp.moveaxis(attended, 0, 1).reshape(NEW * REQ, D)
    hidden_state = (residual.reshape(NEW * REQ, D).astype(jnp.float32) + jnp.dot(attended, w_out, preferred_element_type=jnp.float32)).astype(jnp.bfloat16)
    widened = hidden_state.astype(jnp.float32)
    normed = (widened * lax.rsqrt(lax.optimization_barrier(jnp.mean(widened * widened, axis=1, keepdims=True)) + epsilon) * norm_gain.astype(jnp.float32)).astype(jnp.bfloat16)
    token_count = NEW * REQ
    route_ids = expert_ids.reshape(token_count, TOP)
    gate_rows = gate_weights.reshape(token_count, TOP).astype(jnp.float32)
    combined = jnp.zeros((token_count, D), jnp.float32)
    for expert in range(EXPERTS):
        routed = jnp.any(route_ids == expert, axis=1)
        slot_index = jnp.nonzero(routed, size=N_BLK * CAP, fill_value=token_count)[0].astype(jnp.int32)
        picked_rows = jnp.take(normed, jnp.minimum(slot_index, token_count - 1), axis=0)
        gate_part = jnp.dot(picked_rows, w_gate[expert].T, preferred_element_type=jnp.float32)
        up_part = jnp.dot(picked_rows, w_up[expert].T, preferred_element_type=jnp.float32)
        hidden = (jax.nn.silu(gate_part) * up_part).astype(jnp.bfloat16)
        blocks = jnp.transpose(hidden.reshape(N_BLK * CAP, N_BLK, FF // N_BLK), (1, 0, 2))
        down_rows = w_down[expert].reshape(N_BLK, FF // N_BLK, D)
        summed, unused_rows = lax.scan(add_block, jnp.zeros((N_BLK * CAP, D), jnp.float32), (blocks, down_rows))
        output = summed.astype(jnp.bfloat16)
        spread = jnp.zeros((token_count, D), jnp.bfloat16).at[slot_index].set(output, mode='drop')
        weight = lax.optimization_barrier(jnp.sum(jnp.where(route_ids == expert, gate_rows, 0.0), axis=1))
        expert_term = lax.optimization_barrier((weight[:, None] * spread.astype(jnp.float32)).astype(jnp.bfloat16))
        combined = combined + jnp.where(routed[:, None], expert_term.astype(jnp.float32), 0.0)
    return (widened + combined).astype(jnp.bfloat16).reshape(NEW, REQ, D)
```

```python
import jax
import jax.numpy as jnp
from jax import lax
from jax.experimental import pallas as pl
from jax.experimental.pallas import tpu as pltpu
from jax.sharding import PartitionSpec as P

HEADS = 36
CAP = 136
epsilon = 1e-05
MESH = pl.DeviceIdType.MESH
LANES = 128
CHUNK = 512
TILE = 128
masked_score = -1e30


def attend_kernel(
    q_ref, kn_ref, vn_ref, ck_ref, cv_ref, len_ref, res_ref, gain_ref, w_ref,
    hid_ref, norm_ref,
    qb, kc, kn, vc, vn, qe, kce, kne, vce, vne, sc, bias, ob, oe, att, wv,
    ss, rs, sse, rse, ssq, rsq, lsem, sso, rso, ssoe, rsoe, wsem,
):
    b = lax.axis_index("blk")
    n_blk = 16
    new_span = q_ref.shape[0]
    cache_span = ck_ref.shape[0]
    score_scale = 0.125
    half = b // 8
    quarter = (b // 2) % 4
    core = b % 2

    def dev(j):
        return {"blk": j}

    bar = pltpu.get_barrier_semaphore()
    for k in range(1, n_blk):
        pl.semaphore_signal(bar, inc=1, device_id=dev((b + k) % n_blk), device_id_type=MESH)
    wcopy = pltpu.make_async_copy(w_ref, wv, wsem)
    wcopy.start()
    pl.semaphore_wait(bar, n_blk - 1)

    srcs = (q_ref, ck_ref, kn_ref, cv_ref, vn_ref)
    mains = (qb, kc, kn, vc, vn)
    extras = (None, kce, kne, vce, vne)

    def lane(j):
        return pl.ds(pl.multiple_of(j * LANES, LANES), LANES)

    def rows(j, n):
        return pl.ds(pl.multiple_of(j * n, n), n)

    sends = []
    for a in range(5):
        n = srcs[a].shape[0]
        for k in range(1, n_blk):
            j = (b + k) % n_blk
            c = pltpu.make_async_remote_copy(
                src_ref=srcs[a].at[:, lane(j)], dst_ref=mains[a].at[rows(b, n)],
                send_sem=ss.at[a, k], recv_sem=rs.at[a, k], device_id=dev(j), device_id_type=MESH)
            c.start()
            sends.append(c)
    locals_ = []
    for a in range(5):
        n = srcs[a].shape[0]
        c = pltpu.make_async_copy(srcs[a].at[:, lane(b)], mains[a].at[rows(b, n)], lsem.at[a])
        c.start()
        locals_.append(c)
    esends = []
    for m in range(1, 8):
        j = 2 * ((b // 2 + m) % 8)
        for a in range(1, 5):
            n = srcs[a].shape[0]
            c = pltpu.make_async_remote_copy(
                src_ref=srcs[a].at[:, lane(16 + j // 8)], dst_ref=extras[a].at[rows(b, n)],
                send_sem=sse.at[a - 1, m], recv_sem=rse.at[a - 1, b], device_id=dev(j), device_id_type=MESH)
            c.start()
            esends.append(c)

    def own_remote(a):
        n = srcs[a].shape[0]
        return pltpu.make_async_remote_copy(
            src_ref=srcs[a].at[:, lane(16 + half)], dst_ref=extras[a].at[rows(b, n)],
            send_sem=sse.at[a - 1, 0], recv_sem=rse.at[a - 1, b], device_id=dev(b - 1), device_id_type=MESH)

    def own_local(a):
        n = srcs[a].shape[0]
        return pltpu.make_async_copy(
            srcs[a].at[:, lane(16 + half)], extras[a].at[rows(b, n)], lsem.at[4 + a])

    def q_remote(y):
        j = y * 8 + 2 * (b // 4)
        return pltpu.make_async_remote_copy(
            src_ref=q_ref.at[:, lane(16 + y)], dst_ref=qe.at[rows(b % 4, new_span)],
            send_sem=ssq.at[y], recv_sem=rsq.at[b % 4], device_id=dev(j), device_id_type=MESH)

    def q_local(y):
        return pltpu.make_async_copy(
            q_ref.at[:, lane(16 + y)], qe.at[rows(b % 4, new_span)], lsem.at[9 + y])

    @pl.when(core == 1)
    def _():
        for a in range(1, 5):
            own_remote(a).start()

    @pl.when(core == 0)
    def _():
        for a in range(1, 5):
            own_local(a).start()

    for y in range(2):
        j = y * 8 + 2 * (b // 4)

        @pl.when(j != b)
        def _():
            q_remote(y).start()

        @pl.when(j == b)
        def _():
            q_local(y).start()

    columns = lax.broadcasted_iota(jnp.int32, (1, bias.shape[1]), 1)
    bias[...] = jnp.where(columns < len_ref[0], 0.0, masked_score)

    for c in locals_:
        c.wait()
    for a in range(5):
        for k in range(1, n_blk):
            pltpu.make_async_remote_copy(
                src_ref=srcs[a].at[:, lane(b)], dst_ref=mains[a].at[rows(b, srcs[a].shape[0])],
                send_sem=ss.at[a, k], recv_sem=rs.at[a, k], device_id=dev(b), device_id_type=MESH).wait_recv()

    lane_index = lax.broadcasted_iota(jnp.int32, (TILE, LANES), 1)
    low_half = lane_index < 64

    def tile(q, row0, p0, keys_c, keys_n, vals_c, vals_n, new_chunks, out, cached_chunks=4):
        qt = q[pl.ds(pl.multiple_of(row0, TILE), TILE), :].astype(jnp.float32) * score_scale
        zero = jnp.zeros_like(qt)
        stacked = jnp.concatenate(
            [jnp.where(low_half, qt, zero), jnp.where(low_half, zero, qt)], axis=0).astype(jnp.bfloat16)
        best = None
        for c in range(cached_chunks + new_chunks):
            is_new = c >= cached_chunks
            keys = keys_n if is_new else keys_c
            k0 = (c - cached_chunks if is_new else c) * CHUNK
            s = lax.dot_general(
                stacked, keys[k0:k0 + CHUNK, :], (((1,), (1,)), ((), ())), preferred_element_type=jnp.float32)
            if is_new:
                at = lax.broadcasted_iota(jnp.int32, s.shape, 1) + k0
                pos = lax.broadcasted_iota(jnp.int32, s.shape, 0) % TILE + p0
                s = jnp.where(at <= pos, s, masked_score)
            else:
                s = s + bias[:, k0:k0 + CHUNK]
            sc[:, c * CHUNK:(c + 1) * CHUNK] = s
            for g in range(CHUNK // LANES):
                part = s[:, g * LANES:(g + 1) * LANES]
                best = part if best is None else jnp.maximum(best, part)
        top = jnp.max(best, axis=1, keepdims=True)
        total = None
        mixed = None
        for c in range(cached_chunks + new_chunks):
            is_new = c >= cached_chunks
            vals = vals_n if is_new else vals_c
            k0 = (c - cached_chunks if is_new else c) * CHUNK
            w = jnp.exp(sc[:, c * CHUNK:(c + 1) * CHUNK] - top)
            for g in range(CHUNK // LANES):
                part = w[:, g * LANES:(g + 1) * LANES]
                total = part if total is None else total + part
            o = jnp.dot(w.astype(jnp.bfloat16), vals[k0:k0 + CHUNK, :], preferred_element_type=jnp.float32)
            mixed = o if mixed is None else mixed + o
        mixed = mixed / jnp.sum(total, axis=1, keepdims=True)
        out[pl.ds(pl.multiple_of(row0, TILE), TILE), :] = jnp.where(
            low_half, mixed[:TILE], mixed[TILE:]).astype(jnp.bfloat16)

    @pl.loop(0, 4)
    def _(t):
        tile(qb, t * TILE, t * TILE, kc, kn, vc, vn, 1, ob)

    @pl.loop(4, 8)
    def _(t):
        tile(qb, t * TILE, t * TILE, kc, kn, vc, vn, 2, ob)

    def back(k):
        j = (b + k) % n_blk
        return pltpu.make_async_remote_copy(
            src_ref=ob.at[rows(j, new_span)], dst_ref=att.at[:, lane(b)],
            send_sem=sso.at[k], recv_sem=rso.at[k], device_id=dev(j), device_id_type=MESH)

    backs = [back(k) for k in range(1, n_blk)]
    for c in backs:
        c.start()
    home = pltpu.make_async_copy(ob.at[rows(b, new_span)], att.at[:, lane(b)], lsem.at[11])
    home.start()

    def eback(i):
        return pltpu.make_async_remote_copy(
            src_ref=oe.at[rows(i, new_span)], dst_ref=att.at[:, lane(16 + half)],
            send_sem=ssoe.at[i], recv_sem=rsoe.at[half], device_id=dev(4 * quarter + i), device_id_type=MESH)

    def eback_local(i):
        return pltpu.make_async_copy(oe.at[rows(i, new_span)], att.at[:, lane(16 + half)], lsem.at[12])

    @pl.when(core == 0)
    def _():
        for a in range(1, 5):
            own_local(a).wait()
        for y in range(2):
            @pl.when(y * 8 + 2 * (b // 4) == b)
            def _():
                q_local(y).wait()
        for i in range(4):
            @pl.when((4 * quarter + i) != b)
            def _():
                pltpu.make_async_remote_copy(
                    src_ref=q_ref.at[:, lane(16)], dst_ref=qe.at[rows(i, new_span)],
                    send_sem=ssq.at[0], recv_sem=rsq.at[i], device_id=dev(b), device_id_type=MESH).wait_recv()
        for k in range(1, n_blk):
            s = (b + k) % n_blk
            for a in range(1, 5):
                pltpu.make_async_remote_copy(
                    src_ref=srcs[a].at[:, lane(16)], dst_ref=extras[a].at[rows(s, srcs[a].shape[0])],
                    send_sem=sse.at[a - 1, 0], recv_sem=rse.at[a - 1, s], device_id=dev(b),
                    device_id_type=MESH).wait_recv()

        @pl.loop(0, 2)
        def _(t):
            tile(qe, t * TILE, quarter * 256 + t * TILE, kce, kne, vce, vne, 2, oe)

        for i in range(4):
            @pl.when((4 * quarter + i) != b)
            def _():
                eback(i).start()

            @pl.when((4 * quarter + i) == b)
            def _():
                eback_local(i).start()

    home.wait()
    for k in range(1, n_blk):
        pltpu.make_async_remote_copy(
            src_ref=ob.at[rows(b, new_span)], dst_ref=att.at[:, lane(b)],
            send_sem=sso.at[k], recv_sem=rso.at[k], device_id=dev(b), device_id_type=MESH).wait_recv()
    for y in range(2):
        j = y * 8 + 2 * (b // 4)

        @pl.when(j != b)
        def _():
            pltpu.make_async_remote_copy(
                src_ref=oe.at[rows(0, new_span)], dst_ref=att.at[:, lane(16 + y)],
                send_sem=ssoe.at[0], recv_sem=rsoe.at[y], device_id=dev(b), device_id_type=MESH).wait_recv()

        @pl.when(j == b)
        def _():
            pltpu.make_async_copy(oe.at[rows(0, new_span)], att.at[:, lane(16 + y)], lsem.at[12]).wait()

    wcopy.wait()
    width = 768
    squares = jnp.zeros((new_span, 1), jnp.float32)
    for c in range(q_ref.shape[1] // width):
        cols = slice(c * width, (c + 1) * width)
        h = (res_ref[:, cols].astype(jnp.float32)
             + jnp.dot(att[...], wv[:, cols], preferred_element_type=jnp.float32)).astype(jnp.bfloat16)
        hid_ref[:, cols] = h
        wide = h.astype(jnp.float32)
        squares = squares + jnp.sum(wide * wide, axis=1, keepdims=True)
    factor = lax.rsqrt(squares / q_ref.shape[1] + epsilon)
    norm_ref[...] = (hid_ref[...].astype(jnp.float32) * factor * gain_ref[...]).astype(jnp.bfloat16)

    for c in sends + esends + backs:
        c.wait_send()

    @pl.when(core == 1)
    def _():
        for a in range(1, 5):
            own_remote(a).wait_send()

    @pl.when(core == 0)
    def _():
        for i in range(4):
            @pl.when((4 * quarter + i) != b)
            def _():
                eback(i).wait_send()

    for y in range(2):
        @pl.when(y * 8 + 2 * (b // 4) != b)
        def _():
            q_remote(y).wait_send()


def attend(q, kn, vn, ck, cv, length, residual, gain, w_out):
    span, width = q.shape
    cache = ck.shape[0]
    bf = jnp.bfloat16
    dma = pltpu.SemaphoreType.DMA
    vmem = pl.BlockSpec(memory_space=pltpu.VMEM)
    v = lambda *s: pltpu.VMEM(s, bf)
    return pl.pallas_call(
        attend_kernel,
        out_shape=[jax.ShapeDtypeStruct((span, width), bf)] * 2,
        in_specs=[vmem] * 5 + [pl.BlockSpec(memory_space=pltpu.SMEM), vmem, vmem, pl.BlockSpec(memory_space=pl.ANY)],
        out_specs=[vmem] * 2,
        scratch_shapes=[
            v(16 * span, LANES), v(16 * cache, LANES), v(16 * span, LANES), v(16 * cache, LANES), v(16 * span, LANES),
            v(4 * span, LANES), v(16 * cache, LANES), v(16 * span, LANES), v(16 * cache, LANES), v(16 * span, LANES),
            pltpu.VMEM((2 * TILE, 16 * (span + cache)), jnp.float32), pltpu.VMEM((1, 16 * cache), jnp.float32),
            v(16 * span, LANES), v(4 * span, LANES), v(span, width), v(width, width),
            dma((5, 16)), dma((5, 16)), dma((4, 8)), dma((4, 16)), dma((2,)), dma((4,)), dma((13,)),
            dma((16,)), dma((16,)), dma((4,)), dma((2,)), dma,
        ],
        compiler_params=pltpu.CompilerParams(collective_id=0, has_side_effects=True, vmem_limit_bytes=50 * 2**20),
        name="attend",
    )(q, kn, vn, ck, cv, length, residual, gain, w_out)


def shards(
    q_new,
    k_new,
    v_new,
    cache_k,
    cache_v,
    cache_len,
    residual,
    w_out,
    norm_gain,
    expert_ids,
    gate_weights,
    w_gate,
    w_up,
    w_down,
):
    new_span = q_new.shape[0]
    feature_count = q_new.shape[2]
    expert_index = lax.axis_index("expert")
    hidden_state, normed = attend(
        q_new[:, 0, :], k_new[:, 0, :], v_new[:, 0, :], cache_k[:, 0, :], cache_v[:, 0, :], cache_len,
        residual[:, 0, :], norm_gain.reshape(1, feature_count), w_out)
    widened = hidden_state.astype(jnp.float32)
    row_tokens = lax.all_gather(normed[:, None, :], "expert", axis=1, tiled=True)
    token_count = row_tokens.shape[0] * row_tokens.shape[1]
    flat_tokens = row_tokens.reshape(token_count, feature_count)
    route_ids = expert_ids.reshape(token_count, expert_ids.shape[2])
    routed = jnp.any(route_ids == expert_index, axis=1)
    slot_index = jnp.nonzero(routed, size=CAP, fill_value=token_count - 1)[0]
    slot_tokens = jnp.take(flat_tokens, slot_index, axis=0)
    slot_of = jnp.clip(jnp.cumsum(routed.astype(jnp.int32)) - 1, 0, CAP - 1)
    slot_block = lax.all_gather(slot_tokens, "blk", axis=0, tiled=True)
    gate_part = lax.dot_general(
        w_gate[0], slot_block, (((1,), (1,)), ((), ())), preferred_element_type=jnp.float32
    )
    up_part = lax.dot_general(
        w_up[0], slot_block, (((1,), (1,)), ((), ())), preferred_element_type=jnp.float32
    )
    expert_hidden = (jax.nn.silu(gate_part) * up_part).astype(jnp.bfloat16)
    chosen = lax.slice_in_dim(expert_hidden, 0, lax.axis_size("blk") * CAP, axis=1)
    expert_rows = lax.psum_scatter(
        lax.dot_general(
            chosen, w_down[0], (((0,), (0,)), ((), ())), preferred_element_type=jnp.float32
        ).astype(jnp.bfloat16),
        "blk",
        scatter_dimension=0,
        tiled=True,
    )
    picked = jnp.take(expert_rows, slot_of, axis=0)
    weight = jnp.sum(
        jnp.where(route_ids == expert_index, gate_weights.reshape(token_count, -1), 0.0), axis=1
    )
    expert_term = jnp.where(routed[:, None], weight[:, None] * picked.astype(jnp.float32), 0.0)
    combined = lax.psum_scatter(
        expert_term.reshape(new_span, -1, feature_count).astype(jnp.bfloat16),
        "expert",
        scatter_dimension=1,
        tiled=True,
    ).astype(jnp.float32)
    return (widened[:, None, :] + combined).astype(jnp.bfloat16)


def solution(mesh):
    in_specs = (
        P("blk", "expert", None),
        P("blk", "expert", None),
        P("blk", "expert", None),
        P("blk", "expert", None),
        P("blk", "expert", None),
        P("expert"),
        P("blk", "expert", None),
        P(),
        P(),
        P("blk", None, None),
        P("blk", None, None),
        P("expert", "blk", None),
        P("expert", "blk", None),
        P("expert", "blk", None),
    )
    out_specs = P("blk", "expert", None)
    return jax.shard_map(shards, mesh=mesh, in_specs=in_specs, out_specs=out_specs, check_vma=False)
```

```python
import jax
import jax.numpy as jnp
from jax import lax
from jax.experimental import pallas as pl
from jax.experimental.pallas import tpu as pltpu
from jax.sharding import PartitionSpec as P

HEADS = 36
CAP = 136
epsilon = 1e-05
MESH = pl.DeviceIdType.MESH
LANES = 128
CHUNK = 512
TILE = 128
masked_score = -1e30


def attend_kernel(
    q_ref, kn_ref, vn_ref, ck_ref, cv_ref, len_ref, res_ref, gain_ref, w_ref,
    hid_ref, norm_ref,
    qb, kc, kn, vc, vn, qe, kce, kne, vce, vne, sc, bias, ob, oe, att, wv,
    ss, rs, sse, rse, ssq, rsq, lsem, sso, rso, ssoe, rsoe, wsem,
):
    b = lax.axis_index("blk")
    n_blk = 16
    new_span = q_ref.shape[0]
    cache_span = ck_ref.shape[0]
    score_scale = 0.125
    half = b // 8
    quarter = (b // 2) % 4
    core = b % 2

    def dev(j):
        return {"blk": j}

    bar = pltpu.get_barrier_semaphore()
    for k in range(1, n_blk):
        pl.semaphore_signal(bar, inc=1, device_id=dev((b + k) % n_blk), device_id_type=MESH)
    wcopy = pltpu.make_async_copy(w_ref, wv, wsem)
    wcopy.start()
    pl.semaphore_wait(bar, n_blk - 1)

    srcs = (q_ref, ck_ref, kn_ref, cv_ref, vn_ref)
    mains = (qb, kc, kn, vc, vn)
    extras = (None, kce, kne, vce, vne)

    def lane(j):
        return pl.ds(pl.multiple_of(j * LANES, LANES), LANES)

    def rows(j, n):
        return pl.ds(pl.multiple_of(j * n, n), n)

    sends = []
    for a in range(5):
        n = srcs[a].shape[0]
        for k in range(1, n_blk):
            j = (b + k) % n_blk
            c = pltpu.make_async_remote_copy(
                src_ref=srcs[a].at[:, lane(j)], dst_ref=mains[a].at[rows(b, n)],
                send_sem=ss.at[a, k], recv_sem=rs.at[a, k], device_id=dev(j), device_id_type=MESH)
            c.start()
            sends.append(c)
    locals_ = []
    for a in range(5):
        n = srcs[a].shape[0]
        c = pltpu.make_async_copy(srcs[a].at[:, lane(b)], mains[a].at[rows(b, n)], lsem.at[a])
        c.start()
        locals_.append(c)
    esends = []
    for m in range(1, 8):
        j = 2 * ((b // 2 + m) % 8)
        for a in range(1, 5):
            n = srcs[a].shape[0]
            c = pltpu.make_async_remote_copy(
                src_ref=srcs[a].at[:, lane(16 + j // 8)], dst_ref=extras[a].at[rows(b, n)],
                send_sem=sse.at[a - 1, m], recv_sem=rse.at[a - 1, b], device_id=dev(j), device_id_type=MESH)
            c.start()
            esends.append(c)

    def own_remote(a):
        n = srcs[a].shape[0]
        return pltpu.make_async_remote_copy(
            src_ref=srcs[a].at[:, lane(16 + half)], dst_ref=extras[a].at[rows(b, n)],
            send_sem=sse.at[a - 1, 0], recv_sem=rse.at[a - 1, b], device_id=dev(b - 1), device_id_type=MESH)

    def own_local(a):
        n = srcs[a].shape[0]
        return pltpu.make_async_copy(
            srcs[a].at[:, lane(16 + half)], extras[a].at[rows(b, n)], lsem.at[4 + a])

    def q_remote(y):
        j = y * 8 + 2 * (b // 4)
        return pltpu.make_async_remote_copy(
            src_ref=q_ref.at[:, lane(16 + y)], dst_ref=qe.at[rows(b % 4, new_span)],
            send_sem=ssq.at[y], recv_sem=rsq.at[b % 4], device_id=dev(j), device_id_type=MESH)

    def q_local(y):
        return pltpu.make_async_copy(
            q_ref.at[:, lane(16 + y)], qe.at[rows(b % 4, new_span)], lsem.at[9 + y])

    @pl.when(core == 1)
    def _():
        for a in range(1, 5):
            own_remote(a).start()

    @pl.when(core == 0)
    def _():
        for a in range(1, 5):
            own_local(a).start()

    for y in range(2):
        j = y * 8 + 2 * (b // 4)

        @pl.when(j != b)
        def _():
            q_remote(y).start()

        @pl.when(j == b)
        def _():
            q_local(y).start()

    columns = lax.broadcasted_iota(jnp.int32, (1, bias.shape[1]), 1)
    bias[...] = jnp.where(columns < len_ref[0], 0.0, masked_score)

    for c in locals_:
        c.wait()
    for a in range(5):
        for k in range(1, n_blk):
            pltpu.make_async_remote_copy(
                src_ref=srcs[a].at[:, lane(b)], dst_ref=mains[a].at[rows(b, srcs[a].shape[0])],
                send_sem=ss.at[a, k], recv_sem=rs.at[a, k], device_id=dev(b), device_id_type=MESH).wait_recv()

    lane_index = lax.broadcasted_iota(jnp.int32, (TILE, LANES), 1)
    low_half = lane_index < 64

    def tile(q, row0, p0, keys_c, keys_n, vals_c, vals_n, new_chunks, out, cached_chunks=4):
        qt = q[pl.ds(pl.multiple_of(row0, TILE), TILE), :].astype(jnp.float32) * score_scale
        zero = jnp.zeros_like(qt)
        stacked = jnp.concatenate(
            [jnp.where(low_half, qt, zero), jnp.where(low_half, zero, qt)], axis=0).astype(jnp.bfloat16)
        best = None
        for c in range(cached_chunks + new_chunks):
            is_new = c >= cached_chunks
            keys = keys_n if is_new else keys_c
            k0 = (c - cached_chunks if is_new else c) * CHUNK
            s = lax.dot_general(
                stacked, keys[k0:k0 + CHUNK, :], (((1,), (1,)), ((), ())), preferred_element_type=jnp.float32)
            if is_new:
                at = lax.broadcasted_iota(jnp.int32, s.shape, 1) + k0
                pos = lax.broadcasted_iota(jnp.int32, s.shape, 0) % TILE + p0
                s = jnp.where(at <= pos, s, masked_score)
            else:
                s = s + bias[:, k0:k0 + CHUNK]
            sc[:, c * CHUNK:(c + 1) * CHUNK] = s
            for g in range(CHUNK // LANES):
                part = s[:, g * LANES:(g + 1) * LANES]
                best = part if best is None else jnp.maximum(best, part)
        top = jnp.max(best, axis=1, keepdims=True)
        total = None
        mixed = None
        for c in range(cached_chunks + new_chunks):
            is_new = c >= cached_chunks
            vals = vals_n if is_new else vals_c
            k0 = (c - cached_chunks if is_new else c) * CHUNK
            w = jnp.exp(sc[:, c * CHUNK:(c + 1) * CHUNK] - top)
            for g in range(CHUNK // LANES):
                part = w[:, g * LANES:(g + 1) * LANES]
                total = part if total is None else total + part
            o = jnp.dot(w.astype(jnp.bfloat16), vals[k0:k0 + CHUNK, :], preferred_element_type=jnp.float32)
            mixed = o if mixed is None else mixed + o
        mixed = mixed / jnp.sum(total, axis=1, keepdims=True)
        out[pl.ds(pl.multiple_of(row0, TILE), TILE), :] = jnp.where(
            low_half, mixed[:TILE], mixed[TILE:]).astype(jnp.bfloat16)

    @pl.loop(0, 4)
    def _(t):
        tile(qb, t * TILE, t * TILE, kc, kn, vc, vn, 1, ob)

    @pl.loop(4, 8)
    def _(t):
        tile(qb, t * TILE, t * TILE, kc, kn, vc, vn, 2, ob)

    def back(k):
        j = (b + k) % n_blk
        return pltpu.make_async_remote_copy(
            src_ref=ob.at[rows(j, new_span)], dst_ref=att.at[:, lane(b)],
            send_sem=sso.at[k], recv_sem=rso.at[k], device_id=dev(j), device_id_type=MESH)

    backs = [back(k) for k in range(1, n_blk)]
    for c in backs:
        c.start()
    home = pltpu.make_async_copy(ob.at[rows(b, new_span)], att.at[:, lane(b)], lsem.at[11])
    home.start()

    def eback(i):
        return pltpu.make_async_remote_copy(
            src_ref=oe.at[rows(i, new_span)], dst_ref=att.at[:, lane(16 + half)],
            send_sem=ssoe.at[i], recv_sem=rsoe.at[half], device_id=dev(4 * quarter + i), device_id_type=MESH)

    def eback_local(i):
        return pltpu.make_async_copy(oe.at[rows(i, new_span)], att.at[:, lane(16 + half)], lsem.at[12])

    @pl.when(core == 0)
    def _():
        for a in range(1, 5):
            own_local(a).wait()
        for y in range(2):
            @pl.when(y * 8 + 2 * (b // 4) == b)
            def _():
                q_local(y).wait()
        for i in range(4):
            @pl.when((4 * quarter + i) != b)
            def _():
                pltpu.make_async_remote_copy(
                    src_ref=q_ref.at[:, lane(16)], dst_ref=qe.at[rows(i, new_span)],
                    send_sem=ssq.at[0], recv_sem=rsq.at[i], device_id=dev(b), device_id_type=MESH).wait_recv()
        for k in range(1, n_blk):
            s = (b + k) % n_blk
            for a in range(1, 5):
                pltpu.make_async_remote_copy(
                    src_ref=srcs[a].at[:, lane(16)], dst_ref=extras[a].at[rows(s, srcs[a].shape[0])],
                    send_sem=sse.at[a - 1, 0], recv_sem=rse.at[a - 1, s], device_id=dev(b),
                    device_id_type=MESH).wait_recv()

        @pl.loop(0, 2)
        def _(t):
            tile(qe, t * TILE, quarter * 256 + t * TILE, kce, kne, vce, vne, 2, oe)

        for i in range(4):
            @pl.when((4 * quarter + i) != b)
            def _():
                eback(i).start()

            @pl.when((4 * quarter + i) == b)
            def _():
                eback_local(i).start()

    home.wait()
    for k in range(1, n_blk):
        pltpu.make_async_remote_copy(
            src_ref=ob.at[rows(b, new_span)], dst_ref=att.at[:, lane(b)],
            send_sem=sso.at[k], recv_sem=rso.at[k], device_id=dev(b), device_id_type=MESH).wait_recv()
    for y in range(2):
        j = y * 8 + 2 * (b // 4)

        @pl.when(j != b)
        def _():
            pltpu.make_async_remote_copy(
                src_ref=oe.at[rows(0, new_span)], dst_ref=att.at[:, lane(16 + y)],
                send_sem=ssoe.at[0], recv_sem=rsoe.at[y], device_id=dev(b), device_id_type=MESH).wait_recv()

        @pl.when(j == b)
        def _():
            pltpu.make_async_copy(oe.at[rows(0, new_span)], att.at[:, lane(16 + y)], lsem.at[12]).wait()

    wcopy.wait()
    width = 768
    squares = jnp.zeros((new_span, 1), jnp.float32)
    for c in range(q_ref.shape[1] // width):
        cols = slice(c * width, (c + 1) * width)
        h = (res_ref[:, cols].astype(jnp.float32)
             + jnp.dot(att[...], wv[:, cols], preferred_element_type=jnp.float32)).astype(jnp.bfloat16)
        hid_ref[:, cols] = h
        wide = h.astype(jnp.float32)
        squares = squares + jnp.sum(wide * wide, axis=1, keepdims=True)
    factor = lax.rsqrt(squares / q_ref.shape[1] + epsilon)
    norm_ref[...] = (hid_ref[...].astype(jnp.float32) * factor * gain_ref[...]).astype(jnp.bfloat16)

    for c in sends + esends + backs:
        c.wait_send()

    @pl.when(core == 1)
    def _():
        for a in range(1, 5):
            own_remote(a).wait_send()

    @pl.when(core == 0)
    def _():
        for i in range(4):
            @pl.when((4 * quarter + i) != b)
            def _():
                eback(i).wait_send()

    for y in range(2):
        @pl.when(y * 8 + 2 * (b // 4) != b)
        def _():
            q_remote(y).wait_send()


def attend(q, kn, vn, ck, cv, length, residual, gain, w_out):
    span, width = q.shape
    cache = ck.shape[0]
    bf = jnp.bfloat16
    dma = pltpu.SemaphoreType.DMA
    vmem = pl.BlockSpec(memory_space=pltpu.VMEM)
    v = lambda *s: pltpu.VMEM(s, bf)
    return pl.pallas_call(
        attend_kernel,
        out_shape=[jax.ShapeDtypeStruct((span, width), bf)] * 2,
        in_specs=[vmem] * 5 + [pl.BlockSpec(memory_space=pltpu.SMEM), vmem, vmem, pl.BlockSpec(memory_space=pl.ANY)],
        out_specs=[vmem] * 2,
        scratch_shapes=[
            v(16 * span, LANES), v(16 * cache, LANES), v(16 * span, LANES), v(16 * cache, LANES), v(16 * span, LANES),
            v(4 * span, LANES), v(16 * cache, LANES), v(16 * span, LANES), v(16 * cache, LANES), v(16 * span, LANES),
            pltpu.VMEM((2 * TILE, 16 * (span + cache)), jnp.float32), pltpu.VMEM((1, 16 * cache), jnp.float32),
            v(16 * span, LANES), v(4 * span, LANES), v(span, width), v(width, width),
            dma((5, 16)), dma((5, 16)), dma((4, 8)), dma((4, 16)), dma((2,)), dma((4,)), dma((13,)),
            dma((16,)), dma((16,)), dma((4,)), dma((2,)), dma,
        ],
        compiler_params=pltpu.CompilerParams(collective_id=0, has_side_effects=True, vmem_limit_bytes=50 * 2**20),
        name="attend",
    )(q, kn, vn, ck, cv, length, residual, gain, w_out)


def expert_kernel(
    norm_ref, hid_ref, ids_ref, gw_ref, wg_ref, wu_ref, wd_ref,
    out_ref,
    tok, slab, part, sibr, far, near_l, near_r, row_s, row_r, term, efar, enear_l, enear_r, erow_s, erow_r,
    wg, wu, wd, slots, gates,
    ess, ers, bss, brs, fss, frs, pss, prs, rss, rrs, xss, xrs, lsem, wsem,
):
    b = lax.axis_index("blk")
    e = lax.axis_index("expert")
    h, x, core = b // 8, (b // 2) % 4, b % 2
    eh, ez = e // 4, e % 4
    span, width = norm_ref.shape
    requests = tok.shape[0]
    piece = 768
    first_rows = pl.ds(0, 72)
    last_rows = pl.ds(72, CAP - 72)

    def blk_dev(hh, xx, cc):
        return {"blk": hh * 8 + xx * 2 + cc}

    def exp_dev(hh, zz):
        return {"expert": hh * 4 + zz}

    b_right, b_left = blk_dev(h, (x + 1) % 4, core), blk_dev(h, (x + 3) % 4, core)
    b_across, b_sibling = blk_dev(1 - h, x, core), blk_dev(h, x, 1 - core)
    e_right, e_left, e_across = exp_dev(eh, (ez + 1) % 4), exp_dev(eh, (ez + 3) % 4), exp_dev(1 - eh, ez)

    bar = pltpu.get_barrier_semaphore()
    peers = (b_right, b_left, b_across, b_sibling, e_right, e_left, e_across)
    for peer in peers:
        pl.semaphore_signal(bar, inc=1, device_id=peer, device_id_type=MESH)
    wcopies = [pltpu.make_async_copy(s, d, wsem.at[i]) for i, (s, d) in enumerate(((wg_ref, wg), (wu_ref, wu), (wd_ref, wd)))]
    for c in wcopies:
        c.start()
    own = pltpu.make_async_copy(norm_ref, tok.at[e], lsem)
    own.start()
    pl.semaphore_wait(bar, len(peers))

    sent = []

    def post(src, dst, ssem, rsem, device):
        c = pltpu.make_async_remote_copy(
            src_ref=src, dst_ref=dst, send_sem=ssem, recv_sem=rsem, device_id=device, device_id_type=MESH)
        c.start()
        return c

    def send(*what):
        sent.append(post(*what))

    def arrived(dst, ssem, rsem, device):
        pltpu.make_async_remote_copy(
            src_ref=dst, dst_ref=dst, send_sem=ssem, recv_sem=rsem, device_id=device, device_id_type=MESH).wait_recv()

    def egather(i, block, device, rows=None, src=None):
        dst = tok.at[block] if rows is None else tok.at[block, rows]
        send(dst if src is None else src, dst, ess.at[i], ers.at[i], device)

    def egot(i, block, rows=None):
        arrived(tok.at[block] if rows is None else tok.at[block, rows], ess.at[i], ers.at[i], e_across)

    low, high = pl.ds(0, span // 2), pl.ds(span // 2, span // 2)

    def eb(hh, off):
        return hh * 4 + (ez + off) % 4

    egather(0, e, e_across, src=norm_ref)
    egather(1, e, e_right, src=norm_ref)
    egather(2, e, e_left, src=norm_ref)

    ids0, ids1 = ids_ref[:, 0, :], ids_ref[:, 1, :]
    hit0, hit1 = ids0 == e, ids1 == e
    routed = jnp.where(hit0 | hit1, 1.0, 0.0).astype(jnp.float32)
    upto = (lax.broadcasted_iota(jnp.int32, (span, span), 0) <= lax.broadcasted_iota(jnp.int32, (span, span), 1))
    rank = jnp.dot(routed.astype(jnp.bfloat16), jnp.where(upto, 1.0, 0.0).astype(jnp.bfloat16),
                   preferred_element_type=jnp.float32)
    before = (lax.broadcasted_iota(jnp.int32, (requests, requests), 1) < lax.broadcasted_iota(jnp.int32, (requests, requests), 0))
    ahead = jnp.sum(jnp.dot(jnp.where(before, 1.0, 0.0).astype(jnp.bfloat16), routed.astype(jnp.bfloat16),
                            preferred_element_type=jnp.float32), axis=1, keepdims=True)
    slots[...] = jnp.where(routed > 0, rank + ahead - 1.0, -1.0).astype(jnp.int32)
    gates[...] = jnp.where(hit0, gw_ref[:, 0, :], 0.0) + jnp.where(hit1, gw_ref[:, 1, :], 0.0)

    egot(0, eb(1 - eh, 0))
    egather(3, eb(1 - eh, 0), e_right)
    egather(4, eb(1 - eh, 0), e_left)
    egot(1, eb(eh, 3))
    egather(5, eb(eh, 3), e_right, low)
    egot(2, eb(eh, 1))
    egather(6, eb(eh, 1), e_left, high)
    egot(3, eb(1 - eh, 3))
    egather(7, eb(1 - eh, 3), e_right, low)
    egot(4, eb(1 - eh, 1))
    egather(8, eb(1 - eh, 1), e_left, high)
    egot(5, eb(eh, 2), low)
    egot(6, eb(eh, 2), high)
    egot(7, eb(1 - eh, 2), low)
    egot(8, eb(1 - eh, 2), high)
    own.wait()

    def onehot(r):
        at = lax.broadcasted_iota(jnp.int32, (CAP, span), 0)
        return at == slots[r:r + 1, :]

    home = h * 4 + x
    mine = pl.ds(pl.multiple_of(core * CAP, 8), CAP)
    other = pl.ds(pl.multiple_of((1 - core) * CAP, 8), CAP)
    picks = [jnp.where(onehot(r), 1.0, 0.0).astype(jnp.bfloat16) for r in range(requests)]
    for c0 in range(0, width, piece):
        acc = None
        for r in range(requests):
            o = jnp.dot(picks[r], tok[r, :, c0:c0 + piece], preferred_element_type=jnp.float32)
            acc = o if acc is None else acc + o
        slab[home, mine, c0:c0 + piece] = acc.astype(jnp.bfloat16)

    def bb(hh, off):
        return hh * 4 + (x + off) % 4

    def bview(buf, block, rows=None):
        if rows is None:
            return buf.at[block, mine]
        return buf.at[block, pl.ds(pl.multiple_of(core * CAP + rows.start, 8), rows.size)]

    def bgather(i, block, device, rows=None):
        post(bview(slab, block, rows), bview(slab, block, rows), bss.at[i], brs.at[i], device)

    def bgot(i, block, rows=None):
        arrived(bview(slab, block, rows), bss.at[i], brs.at[i], b_across)

    def share(k, block):
        post(bview(slab, block), bview(slab, block), fss.at[k], frs.at[k], b_sibling)

    for c in wcopies:
        c.wait()

    def advance(k):
        if k == 0:
            bgather(1, home, b_right)
            bgather(2, home, b_left)
            bgather(0, home, b_across)
            share(0, home)
        elif k == 1:
            bgot(1, bb(h, 3))
            bgather(5, bb(h, 3), b_right, first_rows)
            share(1, bb(h, 3))
        elif k == 2:
            bgot(2, bb(h, 1))
            bgather(6, bb(h, 1), b_left, last_rows)
            share(2, bb(h, 1))
        elif k == 3:
            bgot(0, bb(1 - h, 0))
            bgather(3, bb(1 - h, 0), b_right)
            bgather(4, bb(1 - h, 0), b_left)
            share(3, bb(1 - h, 0))
        elif k == 4:
            bgot(3, bb(1 - h, 3))
            bgather(7, bb(1 - h, 3), b_right, first_rows)
            share(4, bb(1 - h, 3))
        elif k == 5:
            bgot(4, bb(1 - h, 1))
            bgather(8, bb(1 - h, 1), b_left, last_rows)
            share(5, bb(1 - h, 1))
        elif k == 6:
            bgot(5, bb(h, 2), first_rows)
            bgot(6, bb(h, 2), last_rows)
            share(6, bb(h, 2))
        else:
            bgot(7, bb(1 - h, 2), first_rows)
            bgot(8, bb(1 - h, 2), last_rows)
            share(7, bb(1 - h, 2))

    offsets = (0, 3, 1, 0, 3, 1, 2, 2)
    flips = (0, 0, 0, 1, 1, 1, 0, 1)
    offset_code = sum(o * 4**i for i, o in enumerate(offsets))
    flip_code = sum(o * 2**i for i, o in enumerate(flips))

    def step(k, powers):
        p4, p2 = powers
        for i in range(8):
            @pl.when(k == i)
            def _(i=i):
                advance(i)
        block = ((h + (flip_code // p2) % 2) % 2) * 4 + (x + (offset_code // p4) % 4) % 4
        arrived(slab.at[block, other], fss.at[k], frs.at[k], b_sibling)
        a = slab[block]
        g = lax.dot_general(a, wg[...], (((1,), (1,)), ((), ())), preferred_element_type=jnp.float32)
        u = lax.dot_general(a, wu[...], (((1,), (1,)), ((), ())), preferred_element_type=jnp.float32)
        act = (g / (1.0 + jnp.exp(-g)) * u).astype(jnp.bfloat16)
        for c0 in range(0, width, piece):
            part[block, :, c0:c0 + piece] = jnp.dot(
                act, wd[:, c0:c0 + piece], preferred_element_type=jnp.float32).astype(jnp.bfloat16)
        pltpu.make_async_remote_copy(
            src_ref=part.at[block, other], dst_ref=sibr.at[block], send_sem=pss.at[k], recv_sem=prs.at[k],
            device_id=b_sibling, device_id_type=MESH).start()
        return p4 * 4, p2 * 2

    one = core * 0 + 1
    lax.fori_loop(0, 8, step, (one, one))

    order = {(f, o): k for k, (f, o) in enumerate(zip(flips, offsets))}

    def pair_sum(flip, off):
        block = bb((h + flip) % 2, off)
        k = order[flip, off]
        arrived(sibr.at[block], pss.at[k], prs.at[k], b_sibling)
        return block, part[block, mine, :].astype(jnp.float32) + sibr[block].astype(jnp.float32)

    for flip in (1, 0):
        block, val = pair_sum(flip, 2)
        part[block, mine, :] = val.astype(jnp.bfloat16)
        send(bview(part, block, first_rows), far.at[flip, first_rows], rss.at[flip, 0], rrs.at[flip, 0], b_right)
        send(bview(part, block, last_rows), far.at[flip, last_rows], rss.at[flip, 1], rrs.at[flip, 1], b_left)
    for flip in (1, 0):
        block, val = pair_sum(flip, 1)
        arrived(far.at[flip, first_rows], rss.at[flip, 0], rrs.at[flip, 0], b_left)
        part[block, mine, :] = jnp.concatenate(
            [val[:72] + far[flip, 0:72, :].astype(jnp.float32), val[72:]], axis=0).astype(jnp.bfloat16)
        send(bview(part, block), near_l.at[flip], rss.at[flip, 2], rrs.at[flip, 2], b_right)
        block, val = pair_sum(flip, 3)
        arrived(far.at[flip, last_rows], rss.at[flip, 1], rrs.at[flip, 1], b_right)
        part[block, mine, :] = jnp.concatenate(
            [val[:72], val[72:] + far[flip, 72:CAP, :].astype(jnp.float32)], axis=0).astype(jnp.bfloat16)
        send(bview(part, block), near_r.at[flip], rss.at[flip, 3], rrs.at[flip, 3], b_left)
    summed = None
    for flip in (1, 0):
        block, val = pair_sum(flip, 0)
        arrived(near_l.at[flip], rss.at[flip, 2], rrs.at[flip, 2], b_left)
        arrived(near_r.at[flip], rss.at[flip, 3], rrs.at[flip, 3], b_right)
        val = val + near_l[flip].astype(jnp.float32) + near_r[flip].astype(jnp.float32)
        if flip:
            row_s[...] = val.astype(jnp.bfloat16)
            send(row_s, row_r, rss.at[2, 0], rrs.at[2, 0], b_across)
        else:
            part[block, mine, :] = val.astype(jnp.bfloat16)
            arrived(row_r, rss.at[2, 0], rrs.at[2, 0], b_across)
            summed = (val + row_r[...].astype(jnp.float32)).astype(jnp.bfloat16)

    gate = None
    for r in range(requests):
        g = jnp.sum(jnp.where(onehot(r), gates[r:r + 1, :], 0.0), axis=1, keepdims=True)
        gate = g if gate is None else gate + g
    row_s_value = (gate * summed.astype(jnp.float32)).astype(jnp.bfloat16)
    sibr[0] = row_s_value

    def spread(block):
        at = lax.broadcasted_iota(jnp.int32, (CAP, span), 0)
        pick = jnp.where(at == slots[pl.ds(block, 1), :], 1.0, 0.0).astype(jnp.bfloat16)
        for c0 in range(0, width, piece):
            term[block, :, c0:c0 + piece] = lax.dot_general(
                pick, sibr[0, :, c0:c0 + piece], (((0,), (0,)), ((), ())),
                preferred_element_type=jnp.float32).astype(jnp.bfloat16)
        return block

    for flip in (1, 0):
        block = spread(eb((eh + flip) % 2, 2))
        send(term.at[block, low], efar.at[flip, low], xss.at[flip, 0], xrs.at[flip, 0], e_right)
        send(term.at[block, high], efar.at[flip, high], xss.at[flip, 1], xrs.at[flip, 1], e_left)
    mid = span // 2
    for flip in (1, 0):
        block = spread(eb((eh + flip) % 2, 1))
        arrived(efar.at[flip, low], xss.at[flip, 0], xrs.at[flip, 0], e_left)
        term[block, 0:mid, :] = (term[block, 0:mid, :].astype(jnp.float32)
                                 + efar[flip, 0:mid, :].astype(jnp.float32)).astype(jnp.bfloat16)
        send(term.at[block], enear_l.at[flip], xss.at[flip, 2], xrs.at[flip, 2], e_right)
        block = spread(eb((eh + flip) % 2, 3))
        arrived(efar.at[flip, high], xss.at[flip, 1], xrs.at[flip, 1], e_right)
        term[block, mid:, :] = (term[block, mid:, :].astype(jnp.float32)
                                + efar[flip, mid:, :].astype(jnp.float32)).astype(jnp.bfloat16)
        send(term.at[block], enear_r.at[flip], xss.at[flip, 3], xrs.at[flip, 3], e_left)
    for flip in (1, 0):
        block = spread(eb((eh + flip) % 2, 0))
        arrived(enear_l.at[flip], xss.at[flip, 2], xrs.at[flip, 2], e_left)
        arrived(enear_r.at[flip], xss.at[flip, 3], xrs.at[flip, 3], e_right)
        val = (term[block].astype(jnp.float32) + enear_l[flip].astype(jnp.float32)
               + enear_r[flip].astype(jnp.float32))
        if flip:
            erow_s[...] = val.astype(jnp.bfloat16)
            send(erow_s, erow_r, xss.at[2, 0], xrs.at[2, 0], e_across)
        else:
            arrived(erow_r, xss.at[2, 0], xrs.at[2, 0], e_across)
            out_ref[...] = (hid_ref[...].astype(jnp.float32) + val
                            + erow_r[...].astype(jnp.float32)).astype(jnp.bfloat16)

    for c in sent:
        c.wait_send()
    for i in range(9):
        view = bview(slab, home, None if i < 5 else first_rows if i % 2 else last_rows)
        pltpu.make_async_remote_copy(
            src_ref=view, dst_ref=view, send_sem=bss.at[i], recv_sem=brs.at[i],
            device_id=b_across, device_id_type=MESH).wait_send()
    for k in range(8):
        view = bview(slab, home)
        pltpu.make_async_remote_copy(
            src_ref=view, dst_ref=view, send_sem=fss.at[k], recv_sem=frs.at[k],
            device_id=b_sibling, device_id_type=MESH).wait_send()
        block = bb((h + flips[k]) % 2, offsets[k])
        pltpu.make_async_remote_copy(
            src_ref=part.at[block, other], dst_ref=sibr.at[block], send_sem=pss.at[k], recv_sem=prs.at[k],
            device_id=b_sibling, device_id_type=MESH).wait_send()


def mix_experts(normed, hidden, ids, gate_weights, w_gate, w_up, w_down):
    span, width = normed.shape
    units = w_gate.shape[0]
    requests = ids.shape[0]
    bf = jnp.bfloat16
    dma = pltpu.SemaphoreType.DMA
    vmem = pl.BlockSpec(memory_space=pltpu.VMEM)
    v = lambda *s: pltpu.VMEM(s, bf)
    return pl.pallas_call(
        expert_kernel,
        out_shape=jax.ShapeDtypeStruct((span, width), bf),
        in_specs=[vmem] * 4 + [pl.BlockSpec(memory_space=pl.ANY)] * 3,
        out_specs=vmem,
        scratch_shapes=[
            v(requests, span, width), v(8, 2 * CAP, width), v(8, 2 * CAP, width), v(8, CAP, width),
            v(2, CAP, width), v(2, CAP, width), v(2, CAP, width), v(CAP, width), v(CAP, width),
            v(requests, span, width), v(2, span, width), v(2, span, width), v(2, span, width), v(span, width), v(span, width),
            v(units, width), v(units, width), v(units, width),
            pltpu.VMEM((requests, span), jnp.int32), pltpu.VMEM((requests, span), jnp.float32),
            dma((9,)), dma((9,)), dma((9,)), dma((9,)), dma((8,)), dma((8,)), dma((8,)), dma((8,)),
            dma((3, 4)), dma((3, 4)), dma((3, 4)), dma((3, 4)), dma, dma((3,)),
        ],
        compiler_params=pltpu.CompilerParams(collective_id=1, has_side_effects=True, vmem_limit_bytes=60 * 2**20),
        name="mix_experts",
    )(normed, hidden, ids, gate_weights, w_gate, w_up, w_down)


def shards(
    q_new,
    k_new,
    v_new,
    cache_k,
    cache_v,
    cache_len,
    residual,
    w_out,
    norm_gain,
    expert_ids,
    gate_weights,
    w_gate,
    w_up,
    w_down,
):
    feature_count = q_new.shape[2]
    hidden_state, normed = attend(
        q_new[:, 0, :], k_new[:, 0, :], v_new[:, 0, :], cache_k[:, 0, :], cache_v[:, 0, :], cache_len,
        residual[:, 0, :], norm_gain.reshape(1, feature_count), w_out)
    layer_out = mix_experts(
        normed, hidden_state, jnp.transpose(expert_ids, (1, 2, 0)), jnp.transpose(gate_weights, (1, 2, 0)),
        w_gate[0], w_up[0], w_down[0])
    return layer_out[:, None, :]


def solution(mesh):
    in_specs = (
        P("blk", "expert", None),
        P("blk", "expert", None),
        P("blk", "expert", None),
        P("blk", "expert", None),
        P("blk", "expert", None),
        P("expert"),
        P("blk", "expert", None),
        P(),
        P(),
        P("blk", None, None),
        P("blk", None, None),
        P("expert", "blk", None),
        P("expert", "blk", None),
        P("expert", "blk", None),
    )
    out_specs = P("blk", "expert", None)
    return jax.shard_map(shards, mesh=mesh, in_specs=in_specs, out_specs=out_specs, check_vma=False)
```

```python
import jax
import jax.numpy as jnp
from jax import lax
from jax.experimental import pallas as pl
from jax.experimental.pallas import tpu as pltpu
from jax.sharding import PartitionSpec as P

HEADS = 36
CAP = 136
epsilon = 1e-05
MESH = pl.DeviceIdType.MESH
LANES = 128
CHUNK = 512
TILE = 128
masked_score = -1e30


def attend_kernel(
    q_hbm, kn_hbm, vn_hbm, ck_hbm, cv_hbm, len_ref, res_hbm, gain_ref, w_ref,
    hid_ref, norm_ref,
    q_ref, kn_ref, vn_ref, ck_ref, cv_ref, res_ref, insem,
    qb, kc, kn, vc, vn, qe, kce, kne, vce, vne, sc, bias, ob, oe, att, wv,
    ss, rs, sse, rse, ssq, rsq, lsem, sso, rso, ssoe, rsoe, wsem,
):
    b = lax.axis_index("blk")
    n_blk = 16
    new_span = q_ref.shape[0]
    cache_span = ck_ref.shape[0]
    score_scale = 0.125
    half = b // 8
    quarter = (b // 2) % 4
    core = b % 2

    def dev(j):
        return {"blk": j}

    bar = pltpu.get_barrier_semaphore()
    for k in range(1, n_blk):
        pl.semaphore_signal(bar, inc=1, device_id=dev((b + k) % n_blk), device_id_type=MESH)
    wcopy = pltpu.make_async_copy(w_ref, wv, wsem)
    loads = [pltpu.make_async_copy(s, d, insem.at[i]) for i, (s, d) in enumerate((
        (q_hbm, q_ref), (ck_hbm, ck_ref), (kn_hbm, kn_ref), (cv_hbm, cv_ref), (vn_hbm, vn_ref), (res_hbm, res_ref)))]
    for c in loads:
        c.start()
    wcopy.start()
    pl.semaphore_wait(bar, n_blk - 1)
    for c in loads:
        c.wait()

    srcs = (q_ref, ck_ref, kn_ref, cv_ref, vn_ref)
    mains = (qb, kc, kn, vc, vn)
    extras = (None, kce, kne, vce, vne)

    def lane(j):
        return pl.ds(pl.multiple_of(j * LANES, LANES), LANES)

    def rows(j, n):
        return pl.ds(pl.multiple_of(j * n, n), n)

    sends = []
    for a in range(5):
        n = srcs[a].shape[0]
        for k in range(1, n_blk):
            j = (b + k) % n_blk
            c = pltpu.make_async_remote_copy(
                src_ref=srcs[a].at[:, lane(j)], dst_ref=mains[a].at[rows(b, n)],
                send_sem=ss.at[a, k], recv_sem=rs.at[a, k], device_id=dev(j), device_id_type=MESH)
            c.start()
            sends.append(c)
    locals_ = []
    for a in range(5):
        n = srcs[a].shape[0]
        c = pltpu.make_async_copy(srcs[a].at[:, lane(b)], mains[a].at[rows(b, n)], lsem.at[a])
        c.start()
        locals_.append(c)
    esends = []
    for m in range(1, 8):
        j = 2 * ((b // 2 + m) % 8)
        for a in range(1, 5):
            n = srcs[a].shape[0]
            c = pltpu.make_async_remote_copy(
                src_ref=srcs[a].at[:, lane(16 + j // 8)], dst_ref=extras[a].at[rows(b, n)],
                send_sem=sse.at[a - 1, m], recv_sem=rse.at[a - 1, b], device_id=dev(j), device_id_type=MESH)
            c.start()
            esends.append(c)

    def own_remote(a):
        n = srcs[a].shape[0]
        return pltpu.make_async_remote_copy(
            src_ref=srcs[a].at[:, lane(16 + half)], dst_ref=extras[a].at[rows(b, n)],
            send_sem=sse.at[a - 1, 0], recv_sem=rse.at[a - 1, b], device_id=dev(b - 1), device_id_type=MESH)

    def own_local(a):
        n = srcs[a].shape[0]
        return pltpu.make_async_copy(
            srcs[a].at[:, lane(16 + half)], extras[a].at[rows(b, n)], lsem.at[4 + a])

    def q_remote(y):
        j = y * 8 + 2 * (b // 4)
        return pltpu.make_async_remote_copy(
            src_ref=q_ref.at[:, lane(16 + y)], dst_ref=qe.at[rows(b % 4, new_span)],
            send_sem=ssq.at[y], recv_sem=rsq.at[b % 4], device_id=dev(j), device_id_type=MESH)

    def q_local(y):
        return pltpu.make_async_copy(
            q_ref.at[:, lane(16 + y)], qe.at[rows(b % 4, new_span)], lsem.at[9 + y])

    @pl.when(core == 1)
    def _():
        for a in range(1, 5):
            own_remote(a).start()

    @pl.when(core == 0)
    def _():
        for a in range(1, 5):
            own_local(a).start()

    for y in range(2):
        j = y * 8 + 2 * (b // 4)

        @pl.when(j != b)
        def _():
            q_remote(y).start()

        @pl.when(j == b)
        def _():
            q_local(y).start()

    columns = lax.broadcasted_iota(jnp.int32, (1, bias.shape[1]), 1)
    bias[...] = jnp.where(columns < len_ref[0], 0.0, masked_score)

    for c in locals_:
        c.wait()
    for a in range(5):
        for k in range(1, n_blk):
            pltpu.make_async_remote_copy(
                src_ref=srcs[a].at[:, lane(b)], dst_ref=mains[a].at[rows(b, srcs[a].shape[0])],
                send_sem=ss.at[a, k], recv_sem=rs.at[a, k], device_id=dev(b), device_id_type=MESH).wait_recv()

    lane_index = lax.broadcasted_iota(jnp.int32, (TILE, LANES), 1)
    low_half = lane_index < 64

    def tile(q, row0, p0, keys_c, keys_n, vals_c, vals_n, new_chunks, out, cached_chunks=4):
        qt = q[pl.ds(pl.multiple_of(row0, TILE), TILE), :].astype(jnp.float32) * score_scale
        zero = jnp.zeros_like(qt)
        stacked = jnp.concatenate(
            [jnp.where(low_half, qt, zero), jnp.where(low_half, zero, qt)], axis=0).astype(jnp.bfloat16)
        best = None
        for c in range(cached_chunks + new_chunks):
            is_new = c >= cached_chunks
            keys = keys_n if is_new else keys_c
            k0 = (c - cached_chunks if is_new else c) * CHUNK
            s = lax.dot_general(
                stacked, keys[k0:k0 + CHUNK, :], (((1,), (1,)), ((), ())), preferred_element_type=jnp.float32)
            if is_new:
                at = lax.broadcasted_iota(jnp.int32, s.shape, 1) + k0
                pos = lax.broadcasted_iota(jnp.int32, s.shape, 0) % TILE + p0
                s = jnp.where(at <= pos, s, masked_score)
            else:
                s = s + bias[:, k0:k0 + CHUNK]
            sc[:, c * CHUNK:(c + 1) * CHUNK] = s
            for g in range(CHUNK // LANES):
                part = s[:, g * LANES:(g + 1) * LANES]
                best = part if best is None else jnp.maximum(best, part)
        top = jnp.max(best, axis=1, keepdims=True)
        total = None
        mixed = None
        for c in range(cached_chunks + new_chunks):
            is_new = c >= cached_chunks
            vals = vals_n if is_new else vals_c
            k0 = (c - cached_chunks if is_new else c) * CHUNK
            w = jnp.exp(sc[:, c * CHUNK:(c + 1) * CHUNK] - top)
            for g in range(CHUNK // LANES):
                part = w[:, g * LANES:(g + 1) * LANES]
                total = part if total is None else total + part
            o = jnp.dot(w.astype(jnp.bfloat16), vals[k0:k0 + CHUNK, :], preferred_element_type=jnp.float32)
            mixed = o if mixed is None else mixed + o
        mixed = mixed / jnp.sum(total, axis=1, keepdims=True)
        out[pl.ds(pl.multiple_of(row0, TILE), TILE), :] = jnp.where(
            low_half, mixed[:TILE], mixed[TILE:]).astype(jnp.bfloat16)

    @pl.loop(0, 4)
    def _(t):
        tile(qb, t * TILE, t * TILE, kc, kn, vc, vn, 1, ob)

    @pl.loop(4, 8)
    def _(t):
        tile(qb, t * TILE, t * TILE, kc, kn, vc, vn, 2, ob)

    def back(k):
        j = (b + k) % n_blk
        return pltpu.make_async_remote_copy(
            src_ref=ob.at[rows(j, new_span)], dst_ref=att.at[:, lane(b)],
            send_sem=sso.at[k], recv_sem=rso.at[k], device_id=dev(j), device_id_type=MESH)

    backs = [back(k) for k in range(1, n_blk)]
    for c in backs:
        c.start()
    home = pltpu.make_async_copy(ob.at[rows(b, new_span)], att.at[:, lane(b)], lsem.at[11])
    home.start()

    def eback(i):
        return pltpu.make_async_remote_copy(
            src_ref=oe.at[rows(i, new_span)], dst_ref=att.at[:, lane(16 + half)],
            send_sem=ssoe.at[i], recv_sem=rsoe.at[half], device_id=dev(4 * quarter + i), device_id_type=MESH)

    def eback_local(i):
        return pltpu.make_async_copy(oe.at[rows(i, new_span)], att.at[:, lane(16 + half)], lsem.at[12])

    @pl.when(core == 0)
    def _():
        for a in range(1, 5):
            own_local(a).wait()
        for y in range(2):
            @pl.when(y * 8 + 2 * (b // 4) == b)
            def _():
                q_local(y).wait()
        for i in range(4):
            @pl.when((4 * quarter + i) != b)
            def _():
                pltpu.make_async_remote_copy(
                    src_ref=q_ref.at[:, lane(16)], dst_ref=qe.at[rows(i, new_span)],
                    send_sem=ssq.at[0], recv_sem=rsq.at[i], device_id=dev(b), device_id_type=MESH).wait_recv()
        for k in range(1, n_blk):
            s = (b + k) % n_blk
            for a in range(1, 5):
                pltpu.make_async_remote_copy(
                    src_ref=srcs[a].at[:, lane(16)], dst_ref=extras[a].at[rows(s, srcs[a].shape[0])],
                    send_sem=sse.at[a - 1, 0], recv_sem=rse.at[a - 1, s], device_id=dev(b),
                    device_id_type=MESH).wait_recv()

        @pl.loop(0, 2)
        def _(t):
            tile(qe, t * TILE, quarter * 256 + t * TILE, kce, kne, vce, vne, 2, oe)

        for i in range(4):
            @pl.when((4 * quarter + i) != b)
            def _():
                eback(i).start()

            @pl.when((4 * quarter + i) == b)
            def _():
                eback_local(i).start()

    home.wait()
    for k in range(1, n_blk):
        pltpu.make_async_remote_copy(
            src_ref=ob.at[rows(b, new_span)], dst_ref=att.at[:, lane(b)],
            send_sem=sso.at[k], recv_sem=rso.at[k], device_id=dev(b), device_id_type=MESH).wait_recv()
    for y in range(2):
        j = y * 8 + 2 * (b // 4)

        @pl.when(j != b)
        def _():
            pltpu.make_async_remote_copy(
                src_ref=oe.at[rows(0, new_span)], dst_ref=att.at[:, lane(16 + y)],
                send_sem=ssoe.at[0], recv_sem=rsoe.at[y], device_id=dev(b), device_id_type=MESH).wait_recv()

        @pl.when(j == b)
        def _():
            pltpu.make_async_copy(oe.at[rows(0, new_span)], att.at[:, lane(16 + y)], lsem.at[12]).wait()

    wcopy.wait()
    width = 768
    squares = jnp.zeros((new_span, 1), jnp.float32)
    for c in range(q_ref.shape[1] // width):
        cols = slice(c * width, (c + 1) * width)
        h = (res_ref[:, cols].astype(jnp.float32)
             + jnp.dot(att[...], wv[:, cols], preferred_element_type=jnp.float32)).astype(jnp.bfloat16)
        hid_ref[:, cols] = h
        wide = h.astype(jnp.float32)
        squares = squares + jnp.sum(wide * wide, axis=1, keepdims=True)
    factor = lax.rsqrt(squares / q_ref.shape[1] + epsilon)
    norm_ref[...] = (hid_ref[...].astype(jnp.float32) * factor * gain_ref[...].reshape(1, q_ref.shape[1])).astype(jnp.bfloat16)

    for c in sends + esends + backs:
        c.wait_send()

    @pl.when(core == 1)
    def _():
        for a in range(1, 5):
            own_remote(a).wait_send()

    @pl.when(core == 0)
    def _():
        for i in range(4):
            @pl.when((4 * quarter + i) != b)
            def _():
                eback(i).wait_send()

    for y in range(2):
        @pl.when(y * 8 + 2 * (b // 4) != b)
        def _():
            q_remote(y).wait_send()


def attend(q, kn, vn, ck, cv, length, residual, gain, w_out):
    span, width = q.shape
    cache = ck.shape[0]
    bf = jnp.bfloat16
    dma = pltpu.SemaphoreType.DMA
    vmem = pl.BlockSpec(memory_space=pltpu.VMEM)
    hbm = pl.BlockSpec(memory_space=pl.ANY)
    v = lambda *s: pltpu.VMEM(s, bf)
    return pl.pallas_call(
        attend_kernel,
        out_shape=[jax.ShapeDtypeStruct((span, width), bf)] * 2,
        in_specs=[hbm] * 5 + [pl.BlockSpec(memory_space=pltpu.SMEM), hbm, vmem, hbm],
        out_specs=[vmem] * 2,
        scratch_shapes=[
            v(span, width), v(span, width), v(span, width), v(cache, width), v(cache, width), v(span, width), dma((6,)),
            v(16 * span, LANES), v(16 * cache, LANES), v(16 * span, LANES), v(16 * cache, LANES), v(16 * span, LANES),
            v(4 * span, LANES), v(16 * cache, LANES), v(16 * span, LANES), v(16 * cache, LANES), v(16 * span, LANES),
            pltpu.VMEM((2 * TILE, 16 * (span + cache)), jnp.float32), pltpu.VMEM((1, 16 * cache), jnp.float32),
            v(16 * span, LANES), v(4 * span, LANES), v(span, width), v(width, width),
            dma((5, 16)), dma((5, 16)), dma((4, 8)), dma((4, 16)), dma((2,)), dma((4,)), dma((13,)),
            dma((16,)), dma((16,)), dma((4,)), dma((2,)), dma,
        ],
        compiler_params=pltpu.CompilerParams(collective_id=0, has_side_effects=True, vmem_limit_bytes=62 * 2**20),
        name="attend",
    )(q, kn, vn, ck, cv, length, residual, gain, w_out)


IN_WIDTHS = (256, 512, 768, 768)
OUT_WIDTHS = (768, 768, 512, 256)
HEAD_ROWS = 72


def columns_of(widths, f):
    return slice(sum(widths[:f]), sum(widths[:f + 1]))


def expert_kernel(
    norm_ref, hid_ref, ids_hbm, gw_hbm, wg_hbm, wu_hbm, wd_hbm,
    out_ref,
    tok, slab, wg, wu, part, sibr, ring, term, ering, wd, weighted,
    cross, pick, gacc, uacc, act, ids_ref, gw_ref, slots, gates,
    ess, ers, bss, brs, fss, frs, pss, prs, rss, rrs, xss, xrs, lsem, wsem,
):
    b = lax.axis_index("blk")
    e = lax.axis_index("expert")
    h, x, core = b // 8, (b // 2) % 4, b % 2
    eh, ez = e // 4, e % 4
    span = norm_ref.shape[0]
    pieces = len(IN_WIDTHS)
    requests = tok[0].shape[0]
    in_across_first = (True, True, False, True)
    out_across_last = (True, False, True, True)

    def blk_dev(hh, xx, cc):
        return {"blk": hh * 8 + xx * 2 + cc}

    def exp_dev(hh, zz):
        return {"expert": hh * 4 + zz}

    b_right, b_left = blk_dev(h, (x + 1) % 4, core), blk_dev(h, (x + 3) % 4, core)
    b_across, b_sibling = blk_dev(1 - h, x, core), blk_dev(h, x, 1 - core)
    e_right, e_left, e_across = exp_dev(eh, (ez + 1) % 4), exp_dev(eh, (ez + 3) % 4), exp_dev(1 - eh, ez)

    bar = pltpu.get_barrier_semaphore()
    peers = (b_right, b_left, b_across, b_sibling, e_right, e_left, e_across)
    for peer in peers:
        pl.semaphore_signal(bar, inc=1, device_id=peer, device_id_type=MESH)
    small = [pltpu.make_async_copy(ids_hbm, ids_ref, lsem.at[pieces]), pltpu.make_async_copy(gw_hbm, gw_ref, lsem.at[pieces + 1])]
    for c in small:
        c.start()
    owns = []
    for f in range(pieces):
        owns.append(pltpu.make_async_copy(norm_ref.at[:, columns_of(IN_WIDTHS, f)], tok[f].at[e], lsem.at[f]))
        owns[-1].start()
    wcopies = []
    for f in range(pieces):
        for i, (src, dst, widths) in enumerate(
                ((wg_hbm, wg, IN_WIDTHS), (wu_hbm, wu, IN_WIDTHS), (wd_hbm, wd, OUT_WIDTHS))):
            wcopies.append(pltpu.make_async_copy(src.at[:, columns_of(widths, f)], dst[f], wsem.at[f, i]))
            wcopies[-1].start()
    pl.semaphore_wait(bar, len(peers))

    sent = []

    def remote(src, dst, ssem, rsem, device):
        return pltpu.make_async_remote_copy(
            src_ref=src, dst_ref=dst, send_sem=ssem, recv_sem=rsem, device_id=device, device_id_type=MESH)

    def send(src, dst, ssem, rsem, device):
        c = remote(src, dst, ssem, rsem, device)
        c.start()
        sent.append(c)

    def arrived(dst, ssem, rsem):
        remote(dst, dst, ssem, rsem, b_across).wait_recv()

    mid = span // 2
    low, high = pl.ds(0, mid), pl.ds(mid, mid)

    def eb(flip, off):
        return ((eh + flip) % 2) * 4 + (ez + off) % 4

    def eview(f, block, rows=None):
        return tok[f].at[block] if rows is None else tok[f].at[block, rows]

    def epost(f, i, block, device, rows=None):
        view = eview(f, block, rows)
        remote(view, view, ess.at[f, i], ers.at[f, i], device).start()

    def egot(f, i, block, rows=None):
        arrived(eview(f, block, rows), ess.at[f, i], ers.at[f, i])

    def expert_open(f):
        src = norm_ref.at[:, columns_of(IN_WIDTHS, f)]
        for i, device in enumerate((e_across, e_right, e_left)):
            remote(src, tok[f].at[e], ess.at[f, i], ers.at[f, i], device).start()

    def expert_middle(f):
        egot(f, 0, eb(1, 0))
        epost(f, 3, eb(1, 0), e_right)
        epost(f, 4, eb(1, 0), e_left)
        egot(f, 1, eb(0, 3))
        epost(f, 5, eb(0, 3), e_right, low)
        egot(f, 2, eb(0, 1))
        epost(f, 6, eb(0, 1), e_left, high)

    def expert_close(f):
        egot(f, 3, eb(1, 3))
        epost(f, 7, eb(1, 3), e_right, low)
        egot(f, 4, eb(1, 1))
        epost(f, 8, eb(1, 1), e_left, high)
        egot(f, 5, eb(0, 2), low)
        egot(f, 6, eb(0, 2), high)
        egot(f, 7, eb(1, 2), low)
        egot(f, 8, eb(1, 2), high)

    home = h * 4 + x
    mine = pl.ds(pl.multiple_of(core * CAP, 8), CAP)
    other = pl.ds(pl.multiple_of((1 - core) * CAP, 8), CAP)

    def select(f):
        acc = None
        for r in range(requests):
            o = jnp.dot(pick[r], tok[f][r], preferred_element_type=jnp.float32)
            acc = o if acc is None else acc + o
        slab[f][home, mine, :] = acc.astype(jnp.bfloat16)

    head, tail = pl.ds(0, HEAD_ROWS), pl.ds(HEAD_ROWS, CAP - HEAD_ROWS)

    def bb(flip, off):
        return ((h + flip) % 2) * 4 + (x + off) % 4

    def view_of(buf, f, block, rows=None):
        if rows is None:
            return buf[f].at[block, mine]
        return buf[f].at[block, pl.ds(pl.multiple_of(core * CAP + rows.start, 8), rows.size)]

    def bpost(f, i, block, device, rows=None):
        view = view_of(slab, f, block, rows)
        remote(view, view, bss.at[f, i], brs.at[f, i], device).start()

    def bgot(f, i, block, rows=None):
        arrived(view_of(slab, f, block, rows), bss.at[f, i], brs.at[f, i])

    def share(f, k, block):
        view = view_of(slab, f, block)
        remote(view, view, fss.at[f, k], frs.at[f, k], b_sibling).start()

    def gather(f, stage):
        if stage == 0:
            bpost(f, 1, home, b_right)
            bpost(f, 2, home, b_left)
            bpost(f, 0, home, b_across)
            share(f, 0, home)
        elif stage == 1:
            bgot(f, 1, bb(0, 3))
            bpost(f, 5, bb(0, 3), b_right, head)
            if not in_across_first[f]:
                bpost(f, 3, bb(0, 3), b_across)
            share(f, 1, bb(0, 3))
            bgot(f, 2, bb(0, 1))
            bpost(f, 6, bb(0, 1), b_left, tail)
            if not in_across_first[f]:
                bpost(f, 4, bb(0, 1), b_across)
            share(f, 2, bb(0, 1))
            bgot(f, 0, bb(1, 0))
            if in_across_first[f]:
                bpost(f, 3, bb(1, 0), b_right)
                bpost(f, 4, bb(1, 0), b_left)
            share(f, 3, bb(1, 0))
        elif stage == 2:
            if not in_across_first[f]:
                bgot(f, 5, bb(0, 2), head)
                bgot(f, 6, bb(0, 2), tail)
                bpost(f, 7, bb(0, 2), b_across)
                share(f, 6, bb(0, 2))
            bgot(f, 3, bb(1, 3))
            if in_across_first[f]:
                bpost(f, 7, bb(1, 3), b_right, head)
            share(f, 4, bb(1, 3))
            bgot(f, 4, bb(1, 1))
            if in_across_first[f]:
                bpost(f, 8, bb(1, 1), b_left, tail)
            share(f, 5, bb(1, 1))
            if in_across_first[f]:
                bgot(f, 5, bb(0, 2), head)
                bgot(f, 6, bb(0, 2), tail)
                share(f, 6, bb(0, 2))
        else:
            if in_across_first[f]:
                bgot(f, 7, bb(1, 2), head)
                bgot(f, 8, bb(1, 2), tail)
            else:
                bgot(f, 7, bb(1, 2))
            share(f, 7, bb(1, 2))

    offsets = (0, 3, 1, 0, 3, 1, 2, 2)
    flips = (0, 0, 0, 1, 1, 1, 0, 1)
    offset_code = sum(o * 4**i for i, o in enumerate(offsets))
    flip_code = sum(o * 2**i for i, o in enumerate(flips))
    order = {(f, o): k for k, (f, o) in enumerate(zip(flips, offsets))}

    expert_open(0)

    for c in small:
        c.wait()
    ids0, ids1 = ids_ref[:, 0, :], ids_ref[:, 1, :]
    hit0, hit1 = ids0 == e, ids1 == e
    routed = jnp.where(hit0 | hit1, 1.0, 0.0).astype(jnp.float32)
    upto = (lax.broadcasted_iota(jnp.int32, (span, span), 0) <= lax.broadcasted_iota(jnp.int32, (span, span), 1))
    rank = jnp.dot(routed.astype(jnp.bfloat16), jnp.where(upto, 1.0, 0.0).astype(jnp.bfloat16),
                   preferred_element_type=jnp.float32)
    before = (lax.broadcasted_iota(jnp.int32, (requests, requests), 1) < lax.broadcasted_iota(jnp.int32, (requests, requests), 0))
    ahead = jnp.sum(jnp.dot(jnp.where(before, 1.0, 0.0).astype(jnp.bfloat16), routed.astype(jnp.bfloat16),
                            preferred_element_type=jnp.float32), axis=1, keepdims=True)
    slots[...] = jnp.where(routed > 0, rank + ahead - 1.0, -1.0).astype(jnp.int32)
    gates[...] = jnp.where(hit0, gw_ref[:, 0, :], 0.0) + jnp.where(hit1, gw_ref[:, 1, :], 0.0)
    for r in range(requests):
        at = lax.broadcasted_iota(jnp.int32, (CAP, span), 0)
        pick[r] = jnp.where(at == slots[r:r + 1, :], 1.0, 0.0).astype(jnp.bfloat16)

    one = core * 0 + 1

    def project(f, first, last):
        def step(k, powers):
            p4, p2 = powers
            block = ((h + (flip_code // p2) % 2) % 2) * 4 + (x + (offset_code // p4) % 4) % 4
            arrived(slab[f].at[block, other], fss.at[f, k], frs.at[f, k])
            a = slab[f][block]
            g = lax.dot_general(a, wg[f][...], (((1,), (1,)), ((), ())), preferred_element_type=jnp.float32)
            u = lax.dot_general(a, wu[f][...], (((1,), (1,)), ((), ())), preferred_element_type=jnp.float32)
            if f:
                g = gacc[block] + g
                u = uacc[block] + u
            if f < pieces - 1:
                gacc[block] = g
                uacc[block] = u
            else:
                act[block] = (g / (1.0 + jnp.exp(-g)) * u).astype(jnp.bfloat16)
            return p4 * 4, p2 * 2

        lax.fori_loop(first, last, step, (one * 4**first, one * 2**first))

    expert_middle(0)
    expert_open(1)
    expert_close(0)
    for c in owns:
        c.wait()
    select(0)
    gather(0, 0)
    expert_middle(1)
    expert_open(2)
    gather(0, 1)
    expert_close(1)
    select(1)
    gather(1, 0)
    gather(0, 2)
    expert_middle(2)
    expert_open(3)
    gather(0, 3)
    gather(1, 1)
    for c in wcopies:
        c.wait()
    project(0, 0, 8)
    expert_close(2)
    select(2)
    gather(2, 0)
    gather(1, 2)
    expert_middle(3)
    gather(1, 3)
    gather(2, 1)
    expert_close(3)
    select(3)
    gather(3, 0)
    project(1, 0, 8)
    gather(2, 2)
    gather(3, 1)
    project(2, 0, 7)
    gather(2, 3)
    gather(3, 2)
    project(2, 7, 8)
    project(3, 0, 7)
    gather(3, 3)
    project(3, 7, 8)

    def down(f):
        def step(i, powers):
            p4, p2 = powers
            k = 7 - i
            block = ((h + (flip_code // p2) % 2) % 2) * 4 + (x + (offset_code // p4) % 4) % 4
            part[f][block] = jnp.dot(act[block], wd[f][...], preferred_element_type=jnp.float32).astype(jnp.bfloat16)
            remote(part[f].at[block, other], sibr[f].at[block], pss.at[f, k], prs.at[f, k], b_sibling).start()
            return p4 // 4, p2 // 2

        lax.fori_loop(0, 8, step, (one * 4**7, one * 2**7))

    def wide(value):
        return value.astype(jnp.float32)

    def pair_sum(f, flip, off):
        block = bb(flip, off)
        k = order[flip, off]
        arrived(sibr[f].at[block], pss.at[f, k], prs.at[f, k])
        return block, wide(part[f][block, mine, :]) + wide(sibr[f][block])

    def keep(f, block, val):
        part[f][block, mine, :] = val.astype(jnp.bfloat16)

    def rsend(f, i, src, dst, device):
        send(src, dst, rss.at[f, i], rrs.at[f, i], device)

    def rgot(f, i, dst):
        arrived(dst, rss.at[f, i], rrs.at[f, i])

    FAR, NEAR_L, NEAR_R, ROW_S, ROW_R = 0, 2, 4, 6, 7

    def slot(f, i, rows=None):
        return ring[f].at[i] if rows is None else ring[f].at[i, rows]

    def ring_far(f, flip, block):
        rsend(f, flip * 4, view_of(part, f, block, head), slot(f, FAR + flip, head), b_right)
        rsend(f, flip * 4 + 1, view_of(part, f, block, tail), slot(f, FAR + flip, tail), b_left)

    def ring_near(f, flip, right, right_val, left, left_val):
        rgot(f, flip * 4, slot(f, FAR + flip, head))
        keep(f, right, jnp.concatenate(
            [right_val[:HEAD_ROWS] + wide(ring[f][FAR + flip, :HEAD_ROWS, :]), right_val[HEAD_ROWS:]], axis=0))
        rsend(f, flip * 4 + 2, view_of(part, f, right), slot(f, NEAR_L + flip), b_right)
        rgot(f, flip * 4 + 1, slot(f, FAR + flip, tail))
        keep(f, left, jnp.concatenate(
            [left_val[:HEAD_ROWS], left_val[HEAD_ROWS:] + wide(ring[f][FAR + flip, HEAD_ROWS:, :])], axis=0))
        rsend(f, flip * 4 + 3, view_of(part, f, left), slot(f, NEAR_R + flip), b_left)

    def ring_end(f, flip, val):
        rgot(f, flip * 4 + 2, slot(f, NEAR_L + flip))
        rgot(f, flip * 4 + 3, slot(f, NEAR_R + flip))
        return val + wide(ring[f][NEAR_L + flip]) + wide(ring[f][NEAR_R + flip])

    def weigh(f, val):
        gate = None
        for r in range(requests):
            g = jnp.sum(jnp.where(pick[r] > 0, gates[r:r + 1, :], 0.0), axis=1, keepdims=True)
            gate = g if gate is None else gate + g
        weighted[f][...] = (gate * wide(val.astype(jnp.bfloat16))).astype(jnp.bfloat16)

    def reduce_stage(f, stage):
        if out_across_last[f]:
            if stage == 0:
                for flip in (1, 0):
                    block, val = pair_sum(f, flip, 2)
                    keep(f, block, val)
                    ring_far(f, flip, block)
            elif stage == 1:
                for flip in (1, 0):
                    right, right_val = pair_sum(f, flip, 1)
                    left, left_val = pair_sum(f, flip, 3)
                    ring_near(f, flip, right, right_val, left, left_val)
            elif stage == 2:
                block, val = pair_sum(f, 1, 0)
                ring[f][ROW_S] = ring_end(f, 1, val).astype(jnp.bfloat16)
                rsend(f, 8, slot(f, ROW_S), slot(f, ROW_R), b_across)
            else:
                block, val = pair_sum(f, 0, 0)
                val = ring_end(f, 0, val)
                rgot(f, 8, slot(f, ROW_R))
                weigh(f, val + wide(ring[f][ROW_R]))
        else:
            if stage == 0:
                for off in (2, 3, 1, 0):
                    block, val = pair_sum(f, 1, off)
                    keep(f, block, val)
                    rsend(f, 4 + off if off else 8, view_of(part, f, block), cross.at[(x + off) % 4], b_across)
            elif stage == 1:
                block, val = pair_sum(f, 0, 2)
                rgot(f, 6, cross.at[(x + 2) % 4])
                keep(f, block, val + wide(cross[(x + 2) % 4]))
                ring_far(f, 0, block)
            elif stage == 2:
                left, left_val = pair_sum(f, 0, 3)
                rgot(f, 7, cross.at[(x + 3) % 4])
                right, right_val = pair_sum(f, 0, 1)
                rgot(f, 5, cross.at[(x + 1) % 4])
                ring_near(f, 0, right, right_val + wide(cross[(x + 1) % 4]), left, left_val + wide(cross[(x + 3) % 4]))
            else:
                block, val = pair_sum(f, 0, 0)
                rgot(f, 8, cross.at[x])
                weigh(f, ring_end(f, 0, val + wide(cross[x])))

    def xsend(f, i, src, dst, device):
        send(src, dst, xss.at[f, i], xrs.at[f, i], device)

    def xgot(f, i, dst):
        arrived(dst, xss.at[f, i], xrs.at[f, i])

    def eslot(f, i, rows=None):
        return ering[f].at[i] if rows is None else ering[f].at[i, rows]

    def spread(f, flip, off):
        block = eb(flip, off)
        return block, lax.dot_general(
            pick[block], weighted[f][...], (((0,), (0,)), ((), ())), preferred_element_type=jnp.float32)

    def return_stage(f, stage):
        if stage == 0:
            for flip in (1, 0):
                block, val = spread(f, flip, 2)
                term[f][block] = val.astype(jnp.bfloat16)
                xsend(f, flip * 4, term[f].at[block, low], eslot(f, FAR + flip, low), e_right)
                xsend(f, flip * 4 + 1, term[f].at[block, high], eslot(f, FAR + flip, high), e_left)
        elif stage == 1:
            for flip in (1, 0):
                block, val = spread(f, flip, 1)
                xgot(f, flip * 4, eslot(f, FAR + flip, low))
                term[f][block] = jnp.concatenate(
                    [val[:mid] + wide(ering[f][FAR + flip, :mid, :]), val[mid:]], axis=0).astype(jnp.bfloat16)
                xsend(f, flip * 4 + 2, term[f].at[block], eslot(f, NEAR_L + flip), e_right)
                block, val = spread(f, flip, 3)
                xgot(f, flip * 4 + 1, eslot(f, FAR + flip, high))
                term[f][block] = jnp.concatenate(
                    [val[:mid], val[mid:] + wide(ering[f][FAR + flip, mid:, :])], axis=0).astype(jnp.bfloat16)
                xsend(f, flip * 4 + 3, term[f].at[block], eslot(f, NEAR_R + flip), e_left)
        else:
            flip = 3 - stage
            block, val = spread(f, flip, 0)
            xgot(f, flip * 4 + 2, eslot(f, NEAR_L + flip))
            xgot(f, flip * 4 + 3, eslot(f, NEAR_R + flip))
            val = val + wide(ering[f][NEAR_L + flip]) + wide(ering[f][NEAR_R + flip])
            if flip:
                ering[f][ROW_S] = val.astype(jnp.bfloat16)
                xsend(f, 8, eslot(f, ROW_S), eslot(f, ROW_R), e_across)
            else:
                xgot(f, 8, eslot(f, ROW_R))
                cols = columns_of(OUT_WIDTHS, f)
                out_ref[:, cols] = (wide(hid_ref[:, cols]) + val + wide(ering[f][ROW_R])).astype(jnp.bfloat16)

    down(0)
    reduce_stage(0, 0)
    down(1)
    reduce_stage(1, 0)
    reduce_stage(0, 1)
    down(2)
    reduce_stage(2, 0)
    reduce_stage(1, 1)
    reduce_stage(0, 2)
    down(3)
    reduce_stage(3, 0)
    reduce_stage(2, 1)
    reduce_stage(1, 2)
    reduce_stage(0, 3)
    return_stage(0, 0)
    reduce_stage(3, 1)
    reduce_stage(2, 2)
    return_stage(0, 1)
    reduce_stage(1, 3)
    return_stage(1, 0)
    reduce_stage(3, 2)
    reduce_stage(2, 3)
    return_stage(2, 0)
    return_stage(0, 2)
    return_stage(1, 1)
    reduce_stage(3, 3)
    return_stage(3, 0)
    return_stage(2, 1)
    return_stage(0, 3)
    return_stage(1, 2)
    return_stage(3, 1)
    return_stage(2, 2)
    return_stage(1, 3)
    return_stage(3, 2)
    return_stage(2, 3)
    return_stage(3, 3)

    for c in sent:
        c.wait_send()

    def drained(view, sems):
        remote(view, view, sems, sems, b_across).wait_send()

    for f in range(pieces):
        for i in range(9):
            drained(eview(f, e, None if i < 5 else low), ess.at[f, i])
        for i in range(9 if in_across_first[f] else 8):
            full = i < 5 or (i == 7 and not in_across_first[f])
            drained(view_of(slab, f, home, None if full else head if i % 2 else tail), bss.at[f, i])
        for k in range(8):
            drained(view_of(slab, f, home), fss.at[f, k])
            drained(view_of(part, f, home), pss.at[f, k])


def mix_experts(normed, hidden, ids, gate_weights, w_gate, w_up, w_down):
    span, width = normed.shape
    units = w_gate.shape[0]
    requests = ids.shape[0]
    pieces = len(IN_WIDTHS)
    bf = jnp.bfloat16
    dma = pltpu.SemaphoreType.DMA
    vmem = pl.BlockSpec(memory_space=pltpu.VMEM)
    hbm = pl.BlockSpec(memory_space=pl.ANY)
    v = lambda *s: pltpu.VMEM(s, bf)
    f32 = lambda *s: pltpu.VMEM(s, jnp.float32)
    return pl.pallas_call(
        expert_kernel,
        out_shape=jax.ShapeDtypeStruct((span, width), bf),
        in_specs=[vmem] * 2 + [hbm] * 5,
        out_specs=vmem,
        scratch_shapes=[
            [v(requests, span, w) for w in IN_WIDTHS], [v(8, 2 * CAP, w) for w in IN_WIDTHS],
            [v(units, w) for w in IN_WIDTHS], [v(units, w) for w in IN_WIDTHS],
            [v(8, 2 * CAP, w) for w in OUT_WIDTHS], [v(8, CAP, w) for w in OUT_WIDTHS],
            [v(8, CAP, w) for w in OUT_WIDTHS], [v(requests, span, w) for w in OUT_WIDTHS],
            [v(8, span, w) for w in OUT_WIDTHS], [v(units, w) for w in OUT_WIDTHS], [v(CAP, w) for w in OUT_WIDTHS],
            v(4, CAP, OUT_WIDTHS[1]), v(requests, CAP, span),
            f32(8, 2 * CAP, units), f32(8, 2 * CAP, units), v(8, 2 * CAP, units),
            pltpu.VMEM(ids.shape, jnp.int32), f32(*gate_weights.shape),
            pltpu.VMEM((requests, span), jnp.int32), f32(requests, span),
            dma((pieces, 9)), dma((pieces, 9)), dma((pieces, 9)), dma((pieces, 9)), dma((pieces, 8)), dma((pieces, 8)),
            dma((pieces, 8)), dma((pieces, 8)), dma((pieces, 9)), dma((pieces, 9)), dma((pieces, 9)), dma((pieces, 9)),
            dma((pieces + 2,)), dma((pieces, 3)),
        ],
        compiler_params=pltpu.CompilerParams(collective_id=1, has_side_effects=True, vmem_limit_bytes=62 * 2**20),
        name="mix_experts",
    )(normed, hidden, ids, gate_weights, w_gate, w_up, w_down)


def shards(
    q_new,
    k_new,
    v_new,
    cache_k,
    cache_v,
    cache_len,
    residual,
    w_out,
    norm_gain,
    expert_ids,
    gate_weights,
    w_gate,
    w_up,
    w_down,
):
    hidden_state, normed = attend(
        q_new[:, 0, :], k_new[:, 0, :], v_new[:, 0, :], cache_k[:, 0, :], cache_v[:, 0, :], cache_len,
        residual[:, 0, :], norm_gain, w_out)
    layer_out = mix_experts(
        normed, hidden_state, jnp.transpose(expert_ids, (1, 2, 0)), jnp.transpose(gate_weights, (1, 2, 0)),
        w_gate[0], w_up[0], w_down[0])
    return layer_out[:, None, :]


def solution(mesh):
    in_specs = (
        P("blk", "expert", None),
        P("blk", "expert", None),
        P("blk", "expert", None),
        P("blk", "expert", None),
        P("blk", "expert", None),
        P("expert"),
        P("blk", "expert", None),
        P(),
        P(),
        P("blk", None, None),
        P("blk", None, None),
        P("expert", "blk", None),
        P("expert", "blk", None),
        P("expert", "blk", None),
    )
    out_specs = P("blk", "expert", None)
    return jax.shard_map(shards, mesh=mesh, in_specs=in_specs, out_specs=out_specs, check_vma=False)
```

```python
import jax
import jax.numpy as jnp
from jax import lax
from jax.experimental import pallas as pl
from jax.experimental.pallas import tpu as pltpu
from jax.sharding import PartitionSpec as P

HEADS = 36
CAP = 136
epsilon = 1e-05
MESH = pl.DeviceIdType.MESH
LANES = 128
CHUNK = 512
TILE = 128
masked_score = -1e30


def attend_kernel(
    q_hbm, kn_hbm, vn_hbm, ck_hbm, cv_hbm, len_ref, res_hbm, gain_ref, w_ref,
    hid_ref, norm_ref,
    q_ref, kn_ref, vn_ref, ck_ref, cv_ref, res_ref, insem,
    qb, kc, kn, vc, vn, qe, kce, kne, vce, vne, sc, bias, ob, oe, att, wv,
    ss, rs, sse, rse, ssq, rsq, lsem, sso, rso, ssoe, rsoe, wsem,
):
    b = lax.axis_index("blk")
    n_blk = 16
    new_span = q_ref.shape[0]
    cache_span = ck_ref.shape[0]
    score_scale = 0.125
    half = b // 8
    quarter = (b // 2) % 4
    core = b % 2

    def dev(j):
        return {"blk": j}

    bar = pltpu.get_barrier_semaphore()
    for k in range(1, n_blk):
        pl.semaphore_signal(bar, inc=1, device_id=dev((b + k) % n_blk), device_id_type=MESH)
    wcopy = pltpu.make_async_copy(w_ref, wv, wsem)
    loads = [pltpu.make_async_copy(s, d, insem.at[i]) for i, (s, d) in enumerate((
        (q_hbm, q_ref), (ck_hbm, ck_ref), (kn_hbm, kn_ref), (cv_hbm, cv_ref), (vn_hbm, vn_ref), (res_hbm, res_ref)))]
    for c in loads:
        c.start()
    wcopy.start()
    pl.semaphore_wait(bar, n_blk - 1)
    for c in loads:
        c.wait()

    srcs = (q_ref, ck_ref, kn_ref, cv_ref, vn_ref)
    mains = (qb, kc, kn, vc, vn)
    extras = (None, kce, kne, vce, vne)

    def lane(j):
        return pl.ds(pl.multiple_of(j * LANES, LANES), LANES)

    def rows(j, n):
        return pl.ds(pl.multiple_of(j * n, n), n)

    sends = []
    for a in range(5):
        n = srcs[a].shape[0]
        for k in range(1, n_blk):
            j = (b + k) % n_blk
            c = pltpu.make_async_remote_copy(
                src_ref=srcs[a].at[:, lane(j)], dst_ref=mains[a].at[rows(b, n)],
                send_sem=ss.at[a, k], recv_sem=rs.at[a, k], device_id=dev(j), device_id_type=MESH)
            c.start()
            sends.append(c)
    locals_ = []
    for a in range(5):
        n = srcs[a].shape[0]
        c = pltpu.make_async_copy(srcs[a].at[:, lane(b)], mains[a].at[rows(b, n)], lsem.at[a])
        c.start()
        locals_.append(c)
    esends = []
    for m in range(1, 8):
        j = 2 * ((b // 2 + m) % 8)
        for a in range(1, 5):
            n = srcs[a].shape[0]
            c = pltpu.make_async_remote_copy(
                src_ref=srcs[a].at[:, lane(16 + j // 8)], dst_ref=extras[a].at[rows(b, n)],
                send_sem=sse.at[a - 1, m], recv_sem=rse.at[a - 1, b], device_id=dev(j), device_id_type=MESH)
            c.start()
            esends.append(c)

    def own_remote(a):
        n = srcs[a].shape[0]
        return pltpu.make_async_remote_copy(
            src_ref=srcs[a].at[:, lane(16 + half)], dst_ref=extras[a].at[rows(b, n)],
            send_sem=sse.at[a - 1, 0], recv_sem=rse.at[a - 1, b], device_id=dev(b - 1), device_id_type=MESH)

    def own_local(a):
        n = srcs[a].shape[0]
        return pltpu.make_async_copy(
            srcs[a].at[:, lane(16 + half)], extras[a].at[rows(b, n)], lsem.at[4 + a])

    def q_remote(y):
        j = y * 8 + 2 * (b // 4)
        return pltpu.make_async_remote_copy(
            src_ref=q_ref.at[:, lane(16 + y)], dst_ref=qe.at[rows(b % 4, new_span)],
            send_sem=ssq.at[y], recv_sem=rsq.at[b % 4], device_id=dev(j), device_id_type=MESH)

    def q_local(y):
        return pltpu.make_async_copy(
            q_ref.at[:, lane(16 + y)], qe.at[rows(b % 4, new_span)], lsem.at[9 + y])

    @pl.when(core == 1)
    def _():
        for a in range(1, 5):
            own_remote(a).start()

    @pl.when(core == 0)
    def _():
        for a in range(1, 5):
            own_local(a).start()

    for y in range(2):
        j = y * 8 + 2 * (b // 4)

        @pl.when(j != b)
        def _():
            q_remote(y).start()

        @pl.when(j == b)
        def _():
            q_local(y).start()

    columns = lax.broadcasted_iota(jnp.int32, (1, bias.shape[1]), 1)
    bias[...] = jnp.where(columns < len_ref[0], 0.0, masked_score)

    for c in locals_:
        c.wait()
    for a in range(5):
        for k in range(1, n_blk):
            pltpu.make_async_remote_copy(
                src_ref=srcs[a].at[:, lane(b)], dst_ref=mains[a].at[rows(b, srcs[a].shape[0])],
                send_sem=ss.at[a, k], recv_sem=rs.at[a, k], device_id=dev(b), device_id_type=MESH).wait_recv()

    lane_index = lax.broadcasted_iota(jnp.int32, (TILE, LANES), 1)
    low_half = lane_index < 64

    def tile(q, row0, p0, keys_c, keys_n, vals_c, vals_n, new_chunks, out, cached_chunks=4):
        qt = q[pl.ds(pl.multiple_of(row0, TILE), TILE), :].astype(jnp.float32) * score_scale
        zero = jnp.zeros_like(qt)
        stacked = jnp.concatenate(
            [jnp.where(low_half, qt, zero), jnp.where(low_half, zero, qt)], axis=0).astype(jnp.bfloat16)
        best = None
        for c in range(cached_chunks + new_chunks):
            is_new = c >= cached_chunks
            keys = keys_n if is_new else keys_c
            k0 = (c - cached_chunks if is_new else c) * CHUNK
            s = lax.dot_general(
                stacked, keys[k0:k0 + CHUNK, :], (((1,), (1,)), ((), ())), preferred_element_type=jnp.float32)
            if is_new:
                at = lax.broadcasted_iota(jnp.int32, s.shape, 1) + k0
                pos = lax.broadcasted_iota(jnp.int32, s.shape, 0) % TILE + p0
                s = jnp.where(at <= pos, s, masked_score)
            else:
                s = s + bias[:, k0:k0 + CHUNK]
            sc[:, c * CHUNK:(c + 1) * CHUNK] = s
            for g in range(CHUNK // LANES):
                part = s[:, g * LANES:(g + 1) * LANES]
                best = part if best is None else jnp.maximum(best, part)
        top = jnp.max(best, axis=1, keepdims=True)
        total = None
        mixed = None
        for c in range(cached_chunks + new_chunks):
            is_new = c >= cached_chunks
            vals = vals_n if is_new else vals_c
            k0 = (c - cached_chunks if is_new else c) * CHUNK
            w = jnp.exp(sc[:, c * CHUNK:(c + 1) * CHUNK] - top)
            for g in range(CHUNK // LANES):
                part = w[:, g * LANES:(g + 1) * LANES]
                total = part if total is None else total + part
            o = jnp.dot(w.astype(jnp.bfloat16), vals[k0:k0 + CHUNK, :], preferred_element_type=jnp.float32)
            mixed = o if mixed is None else mixed + o
        mixed = mixed / jnp.sum(total, axis=1, keepdims=True)
        out[pl.ds(pl.multiple_of(row0, TILE), TILE), :] = jnp.where(
            low_half, mixed[:TILE], mixed[TILE:]).astype(jnp.bfloat16)

    @pl.loop(0, 4)
    def _(t):
        tile(qb, t * TILE, t * TILE, kc, kn, vc, vn, 1, ob)

    @pl.loop(4, 8)
    def _(t):
        tile(qb, t * TILE, t * TILE, kc, kn, vc, vn, 2, ob)

    def back(k):
        j = (b + k) % n_blk
        return pltpu.make_async_remote_copy(
            src_ref=ob.at[rows(j, new_span)], dst_ref=att.at[:, lane(b)],
            send_sem=sso.at[k], recv_sem=rso.at[k], device_id=dev(j), device_id_type=MESH)

    backs = [back(k) for k in range(1, n_blk)]
    for c in backs:
        c.start()
    home = pltpu.make_async_copy(ob.at[rows(b, new_span)], att.at[:, lane(b)], lsem.at[11])
    home.start()

    def eback(i):
        return pltpu.make_async_remote_copy(
            src_ref=oe.at[rows(i, new_span)], dst_ref=att.at[:, lane(16 + half)],
            send_sem=ssoe.at[i], recv_sem=rsoe.at[half], device_id=dev(4 * quarter + i), device_id_type=MESH)

    def eback_local(i):
        return pltpu.make_async_copy(oe.at[rows(i, new_span)], att.at[:, lane(16 + half)], lsem.at[12])

    @pl.when(core == 0)
    def _():
        for a in range(1, 5):
            own_local(a).wait()
        for y in range(2):
            @pl.when(y * 8 + 2 * (b // 4) == b)
            def _():
                q_local(y).wait()
        for i in range(4):
            @pl.when((4 * quarter + i) != b)
            def _():
                pltpu.make_async_remote_copy(
                    src_ref=q_ref.at[:, lane(16)], dst_ref=qe.at[rows(i, new_span)],
                    send_sem=ssq.at[0], recv_sem=rsq.at[i], device_id=dev(b), device_id_type=MESH).wait_recv()
        for k in range(1, n_blk):
            s = (b + k) % n_blk
            for a in range(1, 5):
                pltpu.make_async_remote_copy(
                    src_ref=srcs[a].at[:, lane(16)], dst_ref=extras[a].at[rows(s, srcs[a].shape[0])],
                    send_sem=sse.at[a - 1, 0], recv_sem=rse.at[a - 1, s], device_id=dev(b),
                    device_id_type=MESH).wait_recv()

        @pl.loop(0, 2)
        def _(t):
            tile(qe, t * TILE, quarter * 256 + t * TILE, kce, kne, vce, vne, 2, oe)

        for i in range(4):
            @pl.when((4 * quarter + i) != b)
            def _():
                eback(i).start()

            @pl.when((4 * quarter + i) == b)
            def _():
                eback_local(i).start()

    home.wait()
    for k in range(1, n_blk):
        pltpu.make_async_remote_copy(
            src_ref=ob.at[rows(b, new_span)], dst_ref=att.at[:, lane(b)],
            send_sem=sso.at[k], recv_sem=rso.at[k], device_id=dev(b), device_id_type=MESH).wait_recv()
    for y in range(2):
        j = y * 8 + 2 * (b // 4)

        @pl.when(j != b)
        def _():
            pltpu.make_async_remote_copy(
                src_ref=oe.at[rows(0, new_span)], dst_ref=att.at[:, lane(16 + y)],
                send_sem=ssoe.at[0], recv_sem=rsoe.at[y], device_id=dev(b), device_id_type=MESH).wait_recv()

        @pl.when(j == b)
        def _():
            pltpu.make_async_copy(oe.at[rows(0, new_span)], att.at[:, lane(16 + y)], lsem.at[12]).wait()

    wcopy.wait()
    width = 768
    squares = jnp.zeros((new_span, 1), jnp.float32)
    for c in range(q_ref.shape[1] // width):
        cols = slice(c * width, (c + 1) * width)
        h = (res_ref[:, cols].astype(jnp.float32)
             + jnp.dot(att[...], wv[:, cols], preferred_element_type=jnp.float32)).astype(jnp.bfloat16)
        hid_ref[:, cols] = h
        wide = h.astype(jnp.float32)
        squares = squares + jnp.sum(wide * wide, axis=1, keepdims=True)
    factor = lax.rsqrt(squares / q_ref.shape[1] + epsilon)
    norm_ref[...] = (hid_ref[...].astype(jnp.float32) * factor * gain_ref[...].reshape(1, q_ref.shape[1])).astype(jnp.bfloat16)

    for c in sends + esends + backs:
        c.wait_send()

    @pl.when(core == 1)
    def _():
        for a in range(1, 5):
            own_remote(a).wait_send()

    @pl.when(core == 0)
    def _():
        for i in range(4):
            @pl.when((4 * quarter + i) != b)
            def _():
                eback(i).wait_send()

    for y in range(2):
        @pl.when(y * 8 + 2 * (b // 4) != b)
        def _():
            q_remote(y).wait_send()


def attend(q, kn, vn, ck, cv, length, residual, gain, w_out):
    span, width = q.shape
    cache = ck.shape[0]
    bf = jnp.bfloat16
    dma = pltpu.SemaphoreType.DMA
    vmem = pl.BlockSpec(memory_space=pltpu.VMEM)
    hbm = pl.BlockSpec(memory_space=pl.ANY)
    v = lambda *s: pltpu.VMEM(s, bf)
    return pl.pallas_call(
        attend_kernel,
        out_shape=[jax.ShapeDtypeStruct((span, width), bf)] * 2,
        in_specs=[hbm] * 5 + [pl.BlockSpec(memory_space=pltpu.SMEM), hbm, vmem, hbm],
        out_specs=[vmem] * 2,
        scratch_shapes=[
            v(span, width), v(span, width), v(span, width), v(cache, width), v(cache, width), v(span, width), dma((6,)),
            v(16 * span, LANES), v(16 * cache, LANES), v(16 * span, LANES), v(16 * cache, LANES), v(16 * span, LANES),
            v(4 * span, LANES), v(16 * cache, LANES), v(16 * span, LANES), v(16 * cache, LANES), v(16 * span, LANES),
            pltpu.VMEM((2 * TILE, 16 * (span + cache)), jnp.float32), pltpu.VMEM((1, 16 * cache), jnp.float32),
            v(16 * span, LANES), v(4 * span, LANES), v(span, width), v(width, width),
            dma((5, 16)), dma((5, 16)), dma((4, 8)), dma((4, 16)), dma((2,)), dma((4,)), dma((13,)),
            dma((16,)), dma((16,)), dma((4,)), dma((2,)), dma,
        ],
        compiler_params=pltpu.CompilerParams(collective_id=0, has_side_effects=True, vmem_limit_bytes=62 * 2**20),
        name="attend",
    )(q, kn, vn, ck, cv, length, residual, gain, w_out)


IN_WIDTHS = (768, 768, 768)
OUT_WIDTHS = (768, 768, 512, 256)
HEAD_ROWS = 72


def columns_of(widths, f):
    return slice(sum(widths[:f]), sum(widths[:f + 1]))


def expert_kernel(
    norm_ref, hid_ref, ids_hbm, gw_hbm, wg_hbm, wu_hbm, wd_hbm,
    out_ref,
    tok, slab, wg, wu, part, sibr, ring, term, ering, wd, weighted,
    cross, pick, gacc, uacc, act, ids_ref, gw_ref, slots, gates,
    ess, ers, bss, brs, fss, frs, pss, prs, rss, rrs, xss, xrs, lsem, wsem,
):
    b = lax.axis_index("blk")
    e = lax.axis_index("expert")
    h, x, core = b // 8, (b // 2) % 4, b % 2
    eh, ez = e // 4, e % 4
    span = norm_ref.shape[0]
    pieces = len(IN_WIDTHS)
    requests = tok[0].shape[0]
    in_across_first = (True, False, True)
    out_across_last = (True, False, True, True)

    def blk_dev(hh, xx, cc):
        return {"blk": hh * 8 + xx * 2 + cc}

    def exp_dev(hh, zz):
        return {"expert": hh * 4 + zz}

    b_right, b_left = blk_dev(h, (x + 1) % 4, core), blk_dev(h, (x + 3) % 4, core)
    b_across, b_sibling = blk_dev(1 - h, x, core), blk_dev(h, x, 1 - core)
    e_right, e_left, e_across = exp_dev(eh, (ez + 1) % 4), exp_dev(eh, (ez + 3) % 4), exp_dev(1 - eh, ez)

    bar = pltpu.get_barrier_semaphore()
    peers = (b_right, b_left, b_across, b_sibling, e_right, e_left, e_across)
    for peer in peers:
        pl.semaphore_signal(bar, inc=1, device_id=peer, device_id_type=MESH)
    small = [pltpu.make_async_copy(ids_hbm, ids_ref, lsem.at[pieces]), pltpu.make_async_copy(gw_hbm, gw_ref, lsem.at[pieces + 1])]
    for c in small:
        c.start()
    owns = []
    for f in range(pieces):
        owns.append(pltpu.make_async_copy(norm_ref.at[:, columns_of(IN_WIDTHS, f)], tok[f].at[e], lsem.at[f]))
        owns[-1].start()
    wcopies = []
    for i, (src, dst, widths) in enumerate(
            ((wg_hbm, wg, IN_WIDTHS), (wu_hbm, wu, IN_WIDTHS), (wd_hbm, wd, OUT_WIDTHS))):
        for f in range(len(widths)):
            wcopies.append(pltpu.make_async_copy(src.at[:, columns_of(widths, f)], dst[f], wsem.at[f, i]))
            wcopies[-1].start()
    pl.semaphore_wait(bar, len(peers))

    sent = []

    def remote(src, dst, ssem, rsem, device):
        return pltpu.make_async_remote_copy(
            src_ref=src, dst_ref=dst, send_sem=ssem, recv_sem=rsem, device_id=device, device_id_type=MESH)

    def send(src, dst, ssem, rsem, device):
        c = remote(src, dst, ssem, rsem, device)
        c.start()
        sent.append(c)

    def arrived(dst, ssem, rsem):
        remote(dst, dst, ssem, rsem, b_across).wait_recv()

    mid = span // 2
    low, high = pl.ds(0, mid), pl.ds(mid, mid)

    def eb(flip, off):
        return ((eh + flip) % 2) * 4 + (ez + off) % 4

    def eview(f, block, rows=None):
        return tok[f].at[block] if rows is None else tok[f].at[block, rows]

    def epost(f, i, block, device, rows=None):
        view = eview(f, block, rows)
        remote(view, view, ess.at[f, i], ers.at[f, i], device).start()

    def egot(f, i, block, rows=None):
        arrived(eview(f, block, rows), ess.at[f, i], ers.at[f, i])

    def expert_open(f):
        src = norm_ref.at[:, columns_of(IN_WIDTHS, f)]
        for i, device in enumerate((e_across, e_right, e_left)):
            remote(src, tok[f].at[e], ess.at[f, i], ers.at[f, i], device).start()

    def expert_middle(f):
        egot(f, 0, eb(1, 0))
        epost(f, 3, eb(1, 0), e_right)
        epost(f, 4, eb(1, 0), e_left)
        egot(f, 1, eb(0, 3))
        epost(f, 5, eb(0, 3), e_right, low)
        egot(f, 2, eb(0, 1))
        epost(f, 6, eb(0, 1), e_left, high)

    def expert_close(f):
        egot(f, 3, eb(1, 3))
        epost(f, 7, eb(1, 3), e_right, low)
        egot(f, 4, eb(1, 1))
        epost(f, 8, eb(1, 1), e_left, high)
        egot(f, 5, eb(0, 2), low)
        egot(f, 6, eb(0, 2), high)
        egot(f, 7, eb(1, 2), low)
        egot(f, 8, eb(1, 2), high)

    home = h * 4 + x
    mine = pl.ds(pl.multiple_of(core * CAP, 8), CAP)
    other = pl.ds(pl.multiple_of((1 - core) * CAP, 8), CAP)

    def select(f):
        acc = None
        for r in range(requests):
            o = jnp.dot(pick[r], tok[f][r], preferred_element_type=jnp.float32)
            acc = o if acc is None else acc + o
        slab[f][home, mine, :] = acc.astype(jnp.bfloat16)

    head, tail = pl.ds(0, HEAD_ROWS), pl.ds(HEAD_ROWS, CAP - HEAD_ROWS)

    def bb(flip, off):
        return ((h + flip) % 2) * 4 + (x + off) % 4

    def view_of(buf, f, block, rows=None):
        if rows is None:
            return buf[f].at[block, mine]
        return buf[f].at[block, pl.ds(pl.multiple_of(core * CAP + rows.start, 8), rows.size)]

    def bpost(f, i, block, device, rows=None):
        view = view_of(slab, f, block, rows)
        remote(view, view, bss.at[f, i], brs.at[f, i], device).start()

    def bgot(f, i, block, rows=None):
        arrived(view_of(slab, f, block, rows), bss.at[f, i], brs.at[f, i])

    def share(f, k, block):
        view = view_of(slab, f, block)
        remote(view, view, fss.at[f, k], frs.at[f, k], b_sibling).start()

    def gather(f, stage):
        if stage == 0:
            bpost(f, 1, home, b_right)
            bpost(f, 2, home, b_left)
            bpost(f, 0, home, b_across)
            share(f, 0, home)
        elif stage == 1:
            bgot(f, 1, bb(0, 3))
            bpost(f, 5, bb(0, 3), b_right, head)
            if not in_across_first[f]:
                bpost(f, 3, bb(0, 3), b_across)
            share(f, 1, bb(0, 3))
            bgot(f, 2, bb(0, 1))
            bpost(f, 6, bb(0, 1), b_left, tail)
            if not in_across_first[f]:
                bpost(f, 4, bb(0, 1), b_across)
            share(f, 2, bb(0, 1))
            bgot(f, 0, bb(1, 0))
            if in_across_first[f]:
                bpost(f, 3, bb(1, 0), b_right)
                bpost(f, 4, bb(1, 0), b_left)
            share(f, 3, bb(1, 0))
        elif stage == 2:
            if not in_across_first[f]:
                bgot(f, 5, bb(0, 2), head)
                bgot(f, 6, bb(0, 2), tail)
                bpost(f, 7, bb(0, 2), b_across)
                share(f, 6, bb(0, 2))
            bgot(f, 3, bb(1, 3))
            if in_across_first[f]:
                bpost(f, 7, bb(1, 3), b_right, head)
            share(f, 4, bb(1, 3))
            bgot(f, 4, bb(1, 1))
            if in_across_first[f]:
                bpost(f, 8, bb(1, 1), b_left, tail)
            share(f, 5, bb(1, 1))
            if in_across_first[f]:
                bgot(f, 5, bb(0, 2), head)
                bgot(f, 6, bb(0, 2), tail)
                share(f, 6, bb(0, 2))
        else:
            if in_across_first[f]:
                bgot(f, 7, bb(1, 2), head)
                bgot(f, 8, bb(1, 2), tail)
            else:
                bgot(f, 7, bb(1, 2))
            share(f, 7, bb(1, 2))

    offsets = (0, 3, 1, 0, 3, 1, 2, 2)
    flips = (0, 0, 0, 1, 1, 1, 0, 1)
    offset_code = sum(o * 4**i for i, o in enumerate(offsets))
    flip_code = sum(o * 2**i for i, o in enumerate(flips))
    order = {(f, o): k for k, (f, o) in enumerate(zip(flips, offsets))}

    expert_open(0)

    for c in small:
        c.wait()
    ids0, ids1 = ids_ref[:, 0, :], ids_ref[:, 1, :]
    hit0, hit1 = ids0 == e, ids1 == e
    routed = jnp.where(hit0 | hit1, 1.0, 0.0).astype(jnp.float32)
    upto = (lax.broadcasted_iota(jnp.int32, (span, span), 0) <= lax.broadcasted_iota(jnp.int32, (span, span), 1))
    rank = jnp.dot(routed.astype(jnp.bfloat16), jnp.where(upto, 1.0, 0.0).astype(jnp.bfloat16),
                   preferred_element_type=jnp.float32)
    before = (lax.broadcasted_iota(jnp.int32, (requests, requests), 1) < lax.broadcasted_iota(jnp.int32, (requests, requests), 0))
    ahead = jnp.sum(jnp.dot(jnp.where(before, 1.0, 0.0).astype(jnp.bfloat16), routed.astype(jnp.bfloat16),
                            preferred_element_type=jnp.float32), axis=1, keepdims=True)
    slots[...] = jnp.where(routed > 0, rank + ahead - 1.0, -1.0).astype(jnp.int32)
    gates[...] = jnp.where(hit0, gw_ref[:, 0, :], 0.0) + jnp.where(hit1, gw_ref[:, 1, :], 0.0)
    for r in range(requests):
        at = lax.broadcasted_iota(jnp.int32, (CAP, span), 0)
        pick[r] = jnp.where(at == slots[r:r + 1, :], 1.0, 0.0).astype(jnp.bfloat16)

    one = core * 0 + 1

    def project(f, first, last):
        def step(k, powers):
            p4, p2 = powers
            block = ((h + (flip_code // p2) % 2) % 2) * 4 + (x + (offset_code // p4) % 4) % 4
            arrived(slab[f].at[block, other], fss.at[f, k], frs.at[f, k])
            a = slab[f][block]
            g = lax.dot_general(a, wg[f][...], (((1,), (1,)), ((), ())), preferred_element_type=jnp.float32)
            u = lax.dot_general(a, wu[f][...], (((1,), (1,)), ((), ())), preferred_element_type=jnp.float32)
            if f:
                g = gacc[block] + g
                u = uacc[block] + u
            if f < pieces - 1:
                gacc[block] = g
                uacc[block] = u
            else:
                act[block] = (g / (1.0 + jnp.exp(-g)) * u).astype(jnp.bfloat16)
            return p4 * 4, p2 * 2

        lax.fori_loop(first, last, step, (one * 4**first, one * 2**first))

    expert_middle(0)
    expert_open(1)
    expert_close(0)
    for c in owns:
        c.wait()
    select(0)
    gather(0, 0)
    expert_middle(1)
    expert_open(2)
    expert_close(1)
    select(1)
    gather(1, 0)
    gather(0, 1)
    expert_middle(2)
    expert_close(2)
    select(2)
    gather(2, 0)
    gather(0, 2)
    gather(1, 1)
    gather(0, 3)
    gather(1, 2)
    gather(2, 1)
    for c in wcopies:
        c.wait()
    project(0, 0, 8)
    gather(1, 3)
    gather(2, 2)
    project(1, 0, 8)
    project(2, 0, 7)
    gather(2, 3)
    project(2, 7, 8)

    def down(f):
        def step(i, powers):
            p4, p2 = powers
            k = 7 - i
            block = ((h + (flip_code // p2) % 2) % 2) * 4 + (x + (offset_code // p4) % 4) % 4
            part[f][block] = jnp.dot(act[block], wd[f][...], preferred_element_type=jnp.float32).astype(jnp.bfloat16)
            remote(part[f].at[block, other], sibr[f].at[block], pss.at[f, k], prs.at[f, k], b_sibling).start()
            return p4 // 4, p2 // 2

        lax.fori_loop(0, 8, step, (one * 4**7, one * 2**7))

    def wide(value):
        return value.astype(jnp.float32)

    def pair_sum(f, flip, off):
        block = bb(flip, off)
        k = order[flip, off]
        arrived(sibr[f].at[block], pss.at[f, k], prs.at[f, k])
        return block, wide(part[f][block, mine, :]) + wide(sibr[f][block])

    def keep(f, block, val):
        part[f][block, mine, :] = val.astype(jnp.bfloat16)

    def rsend(f, i, src, dst, device):
        send(src, dst, rss.at[f, i], rrs.at[f, i], device)

    def rgot(f, i, dst):
        arrived(dst, rss.at[f, i], rrs.at[f, i])

    FAR, NEAR_L, NEAR_R, ROW_S, ROW_R = 0, 2, 4, 6, 7

    def slot(f, i, rows=None):
        return ring[f].at[i] if rows is None else ring[f].at[i, rows]

    def ring_far(f, flip, block):
        rsend(f, flip * 4, view_of(part, f, block, head), slot(f, FAR + flip, head), b_right)
        rsend(f, flip * 4 + 1, view_of(part, f, block, tail), slot(f, FAR + flip, tail), b_left)

    def ring_near(f, flip, right, right_val, left, left_val):
        rgot(f, flip * 4, slot(f, FAR + flip, head))
        keep(f, right, jnp.concatenate(
            [right_val[:HEAD_ROWS] + wide(ring[f][FAR + flip, :HEAD_ROWS, :]), right_val[HEAD_ROWS:]], axis=0))
        rsend(f, flip * 4 + 2, view_of(part, f, right), slot(f, NEAR_L + flip), b_right)
        rgot(f, flip * 4 + 1, slot(f, FAR + flip, tail))
        keep(f, left, jnp.concatenate(
            [left_val[:HEAD_ROWS], left_val[HEAD_ROWS:] + wide(ring[f][FAR + flip, HEAD_ROWS:, :])], axis=0))
        rsend(f, flip * 4 + 3, view_of(part, f, left), slot(f, NEAR_R + flip), b_left)

    def ring_end(f, flip, val):
        rgot(f, flip * 4 + 2, slot(f, NEAR_L + flip))
        rgot(f, flip * 4 + 3, slot(f, NEAR_R + flip))
        return val + wide(ring[f][NEAR_L + flip]) + wide(ring[f][NEAR_R + flip])

    def weigh(f, val):
        gate = None
        for r in range(requests):
            g = jnp.sum(jnp.where(pick[r] > 0, gates[r:r + 1, :], 0.0), axis=1, keepdims=True)
            gate = g if gate is None else gate + g
        weighted[f][...] = (gate * wide(val.astype(jnp.bfloat16))).astype(jnp.bfloat16)

    def reduce_stage(f, stage):
        if out_across_last[f]:
            if stage == 0:
                for flip in (1, 0):
                    block, val = pair_sum(f, flip, 2)
                    keep(f, block, val)
                    ring_far(f, flip, block)
            elif stage == 1:
                for flip in (1, 0):
                    right, right_val = pair_sum(f, flip, 1)
                    left, left_val = pair_sum(f, flip, 3)
                    ring_near(f, flip, right, right_val, left, left_val)
            elif stage == 2:
                block, val = pair_sum(f, 1, 0)
                ring[f][ROW_S] = ring_end(f, 1, val).astype(jnp.bfloat16)
                rsend(f, 8, slot(f, ROW_S), slot(f, ROW_R), b_across)
            else:
                block, val = pair_sum(f, 0, 0)
                val = ring_end(f, 0, val)
                rgot(f, 8, slot(f, ROW_R))
                weigh(f, val + wide(ring[f][ROW_R]))
        else:
            if stage == 0:
                for off in (2, 3, 1, 0):
                    block, val = pair_sum(f, 1, off)
                    keep(f, block, val)
                    rsend(f, 4 + off if off else 8, view_of(part, f, block), cross.at[(x + off) % 4], b_across)
            elif stage == 1:
                block, val = pair_sum(f, 0, 2)
                rgot(f, 6, cross.at[(x + 2) % 4])
                keep(f, block, val + wide(cross[(x + 2) % 4]))
                ring_far(f, 0, block)
            elif stage == 2:
                left, left_val = pair_sum(f, 0, 3)
                rgot(f, 7, cross.at[(x + 3) % 4])
                right, right_val = pair_sum(f, 0, 1)
                rgot(f, 5, cross.at[(x + 1) % 4])
                ring_near(f, 0, right, right_val + wide(cross[(x + 1) % 4]), left, left_val + wide(cross[(x + 3) % 4]))
            else:
                block, val = pair_sum(f, 0, 0)
                rgot(f, 8, cross.at[x])
                weigh(f, ring_end(f, 0, val + wide(cross[x])))

    def xsend(f, i, src, dst, device):
        send(src, dst, xss.at[f, i], xrs.at[f, i], device)

    def xgot(f, i, dst):
        arrived(dst, xss.at[f, i], xrs.at[f, i])

    def eslot(f, i, rows=None):
        return ering[f].at[i] if rows is None else ering[f].at[i, rows]

    def spread(f, flip, off):
        block = eb(flip, off)
        return block, lax.dot_general(
            pick[block], weighted[f][...], (((0,), (0,)), ((), ())), preferred_element_type=jnp.float32)

    def return_stage(f, stage):
        if stage == 0:
            for flip in (1, 0):
                block, val = spread(f, flip, 2)
                term[f][block] = val.astype(jnp.bfloat16)
                xsend(f, flip * 4, term[f].at[block, low], eslot(f, FAR + flip, low), e_right)
                xsend(f, flip * 4 + 1, term[f].at[block, high], eslot(f, FAR + flip, high), e_left)
        elif stage == 1:
            for flip in (1, 0):
                block, val = spread(f, flip, 1)
                xgot(f, flip * 4, eslot(f, FAR + flip, low))
                term[f][block] = jnp.concatenate(
                    [val[:mid] + wide(ering[f][FAR + flip, :mid, :]), val[mid:]], axis=0).astype(jnp.bfloat16)
                xsend(f, flip * 4 + 2, term[f].at[block], eslot(f, NEAR_L + flip), e_right)
                block, val = spread(f, flip, 3)
                xgot(f, flip * 4 + 1, eslot(f, FAR + flip, high))
                term[f][block] = jnp.concatenate(
                    [val[:mid], val[mid:] + wide(ering[f][FAR + flip, mid:, :])], axis=0).astype(jnp.bfloat16)
                xsend(f, flip * 4 + 3, term[f].at[block], eslot(f, NEAR_R + flip), e_left)
        else:
            flip = 3 - stage
            block, val = spread(f, flip, 0)
            xgot(f, flip * 4 + 2, eslot(f, NEAR_L + flip))
            xgot(f, flip * 4 + 3, eslot(f, NEAR_R + flip))
            val = val + wide(ering[f][NEAR_L + flip]) + wide(ering[f][NEAR_R + flip])
            if flip:
                ering[f][ROW_S] = val.astype(jnp.bfloat16)
                xsend(f, 8, eslot(f, ROW_S), eslot(f, ROW_R), e_across)
            else:
                xgot(f, 8, eslot(f, ROW_R))
                cols = columns_of(OUT_WIDTHS, f)
                out_ref[:, cols] = (wide(hid_ref[:, cols]) + val + wide(ering[f][ROW_R])).astype(jnp.bfloat16)

    down(0)
    reduce_stage(0, 0)
    down(1)
    reduce_stage(1, 0)
    reduce_stage(0, 1)
    down(2)
    reduce_stage(2, 0)
    reduce_stage(1, 1)
    reduce_stage(0, 2)
    down(3)
    reduce_stage(3, 0)
    reduce_stage(2, 1)
    reduce_stage(1, 2)
    reduce_stage(0, 3)
    return_stage(0, 0)
    reduce_stage(3, 1)
    reduce_stage(2, 2)
    return_stage(0, 1)
    reduce_stage(1, 3)
    return_stage(1, 0)
    reduce_stage(3, 2)
    reduce_stage(2, 3)
    return_stage(2, 0)
    return_stage(0, 2)
    return_stage(1, 1)
    reduce_stage(3, 3)
    return_stage(3, 0)
    return_stage(2, 1)
    return_stage(0, 3)
    return_stage(1, 2)
    return_stage(3, 1)
    return_stage(2, 2)
    return_stage(1, 3)
    return_stage(3, 2)
    return_stage(2, 3)
    return_stage(3, 3)

    for c in sent:
        c.wait_send()

    def drained(view, sems):
        remote(view, view, sems, sems, b_across).wait_send()

    for f in range(pieces):
        for i in range(9):
            drained(eview(f, e, None if i < 5 else low), ess.at[f, i])
        for i in range(9 if in_across_first[f] else 8):
            full = i < 5 or (i == 7 and not in_across_first[f])
            drained(view_of(slab, f, home, None if full else head if i % 2 else tail), bss.at[f, i])
        for k in range(8):
            drained(view_of(slab, f, home), fss.at[f, k])
    for f in range(len(OUT_WIDTHS)):
        for k in range(8):
            drained(view_of(part, f, home), pss.at[f, k])


def mix_experts(normed, hidden, ids, gate_weights, w_gate, w_up, w_down):
    span, width = normed.shape
    units = w_gate.shape[0]
    requests = ids.shape[0]
    pieces = max(len(IN_WIDTHS), len(OUT_WIDTHS))
    bf = jnp.bfloat16
    dma = pltpu.SemaphoreType.DMA
    vmem = pl.BlockSpec(memory_space=pltpu.VMEM)
    hbm = pl.BlockSpec(memory_space=pl.ANY)
    v = lambda *s: pltpu.VMEM(s, bf)
    f32 = lambda *s: pltpu.VMEM(s, jnp.float32)
    return pl.pallas_call(
        expert_kernel,
        out_shape=jax.ShapeDtypeStruct((span, width), bf),
        in_specs=[vmem] * 2 + [hbm] * 5,
        out_specs=vmem,
        scratch_shapes=[
            [v(requests, span, w) for w in IN_WIDTHS], [v(8, 2 * CAP, w) for w in IN_WIDTHS],
            [v(units, w) for w in IN_WIDTHS], [v(units, w) for w in IN_WIDTHS],
            [v(8, 2 * CAP, w) for w in OUT_WIDTHS], [v(8, CAP, w) for w in OUT_WIDTHS],
            [v(8, CAP, w) for w in OUT_WIDTHS], [v(requests, span, w) for w in OUT_WIDTHS],
            [v(8, span, w) for w in OUT_WIDTHS], [v(units, w) for w in OUT_WIDTHS], [v(CAP, w) for w in OUT_WIDTHS],
            v(4, CAP, OUT_WIDTHS[1]), v(requests, CAP, span),
            f32(8, 2 * CAP, units), f32(8, 2 * CAP, units), v(8, 2 * CAP, units),
            pltpu.VMEM(ids.shape, jnp.int32), f32(*gate_weights.shape),
            pltpu.VMEM((requests, span), jnp.int32), f32(requests, span),
            dma((pieces, 9)), dma((pieces, 9)), dma((pieces, 9)), dma((pieces, 9)), dma((pieces, 8)), dma((pieces, 8)),
            dma((pieces, 8)), dma((pieces, 8)), dma((pieces, 9)), dma((pieces, 9)), dma((pieces, 9)), dma((pieces, 9)),
            dma((pieces + 2,)), dma((pieces, 3)),
        ],
        compiler_params=pltpu.CompilerParams(collective_id=1, has_side_effects=True, vmem_limit_bytes=62 * 2**20),
        name="mix_experts",
    )(normed, hidden, ids, gate_weights, w_gate, w_up, w_down)


def shards(
    q_new,
    k_new,
    v_new,
    cache_k,
    cache_v,
    cache_len,
    residual,
    w_out,
    norm_gain,
    expert_ids,
    gate_weights,
    w_gate,
    w_up,
    w_down,
):
    hidden_state, normed = attend(
        q_new[:, 0, :], k_new[:, 0, :], v_new[:, 0, :], cache_k[:, 0, :], cache_v[:, 0, :], cache_len,
        residual[:, 0, :], norm_gain, w_out)
    layer_out = mix_experts(
        normed, hidden_state, jnp.transpose(expert_ids, (1, 2, 0)), jnp.transpose(gate_weights, (1, 2, 0)),
        w_gate[0], w_up[0], w_down[0])
    return layer_out[:, None, :]


def solution(mesh):
    in_specs = (
        P("blk", "expert", None),
        P("blk", "expert", None),
        P("blk", "expert", None),
        P("blk", "expert", None),
        P("blk", "expert", None),
        P("expert"),
        P("blk", "expert", None),
        P(),
        P(),
        P("blk", None, None),
        P("blk", None, None),
        P("expert", "blk", None),
        P("expert", "blk", None),
        P("expert", "blk", None),
    )
    out_specs = P("blk", "expert", None)
    return jax.shard_map(shards, mesh=mesh, in_specs=in_specs, out_specs=out_specs, check_vma=False)
```

```python
import jax
import jax.numpy as jnp
from jax import lax
from jax.experimental import pallas as pl
from jax.experimental.pallas import tpu as pltpu
from jax.sharding import PartitionSpec as P

HEADS = 36
CAP = 136
epsilon = 1e-05
MESH = pl.DeviceIdType.MESH
LANES = 128
CHUNK = 512
TILE = 128
masked_score = -1e30


def attend_kernel(
    q_hbm, kn_hbm, vn_hbm, ck_hbm, cv_hbm, len_ref, res_hbm, gain_ref, w_ref,
    hid_ref, norm_ref,
    q_ref, kn_ref, vn_ref, ck_ref, cv_ref, res_ref, insem,
    qb, kc, kn, vc, vn, qe, kce, kne, vce, vne, sc, tops, bias, ob, oe, att, wv,
    ss, rs, sse, rse, ssq, rsq, lsem, sso, rso, ssoe, rsoe, wsem,
):
    b = lax.axis_index("blk")
    n_blk = 16
    new_span = q_ref.shape[0]
    cache_span = ck_ref.shape[0]
    score_scale = 0.125
    half = b // 8
    quarter = (b // 2) % 4
    core = b % 2

    def dev(j):
        return {"blk": j}

    bar = pltpu.get_barrier_semaphore()
    for k in range(1, n_blk):
        pl.semaphore_signal(bar, inc=1, device_id=dev((b + k) % n_blk), device_id_type=MESH)
    wcopy = pltpu.make_async_copy(w_ref, wv, wsem)
    loads = [pltpu.make_async_copy(s, d, insem.at[i]) for i, (s, d) in enumerate((
        (q_hbm, q_ref), (ck_hbm, ck_ref), (kn_hbm, kn_ref), (cv_hbm, cv_ref), (vn_hbm, vn_ref), (res_hbm, res_ref)))]
    for c in loads:
        c.start()
    wcopy.start()
    pl.semaphore_wait(bar, n_blk - 1)
    for c in loads:
        c.wait()

    srcs = (q_ref, ck_ref, kn_ref, cv_ref, vn_ref)
    mains = (qb, kc, kn, vc, vn)
    extras = (None, kce, kne, vce, vne)

    def lane(j):
        return pl.ds(pl.multiple_of(j * LANES, LANES), LANES)

    def rows(j, n):
        return pl.ds(pl.multiple_of(j * n, n), n)

    sends = []
    for a in range(5):
        n = srcs[a].shape[0]
        for k in range(1, n_blk):
            j = (b + k) % n_blk
            c = pltpu.make_async_remote_copy(
                src_ref=srcs[a].at[:, lane(j)], dst_ref=mains[a].at[rows(b, n)],
                send_sem=ss.at[a, k], recv_sem=rs.at[a, k], device_id=dev(j), device_id_type=MESH)
            c.start()
            sends.append(c)
    locals_ = []
    for a in range(5):
        n = srcs[a].shape[0]
        c = pltpu.make_async_copy(srcs[a].at[:, lane(b)], mains[a].at[rows(b, n)], lsem.at[a])
        c.start()
        locals_.append(c)
    esends = []
    for m in range(1, 8):
        j = 2 * ((b // 2 + m) % 8)
        for a in range(1, 5):
            n = srcs[a].shape[0]
            c = pltpu.make_async_remote_copy(
                src_ref=srcs[a].at[:, lane(16 + j // 8)], dst_ref=extras[a].at[rows(b, n)],
                send_sem=sse.at[a - 1, m], recv_sem=rse.at[a - 1, b], device_id=dev(j), device_id_type=MESH)
            c.start()
            esends.append(c)

    def own_remote(a):
        n = srcs[a].shape[0]
        return pltpu.make_async_remote_copy(
            src_ref=srcs[a].at[:, lane(16 + half)], dst_ref=extras[a].at[rows(b, n)],
            send_sem=sse.at[a - 1, 0], recv_sem=rse.at[a - 1, b], device_id=dev(b - 1), device_id_type=MESH)

    def own_local(a):
        n = srcs[a].shape[0]
        return pltpu.make_async_copy(
            srcs[a].at[:, lane(16 + half)], extras[a].at[rows(b, n)], lsem.at[4 + a])

    def q_remote(y):
        j = y * 8 + 2 * (b // 4)
        return pltpu.make_async_remote_copy(
            src_ref=q_ref.at[:, lane(16 + y)], dst_ref=qe.at[rows(b % 4, new_span)],
            send_sem=ssq.at[y], recv_sem=rsq.at[b % 4], device_id=dev(j), device_id_type=MESH)

    def q_local(y):
        return pltpu.make_async_copy(
            q_ref.at[:, lane(16 + y)], qe.at[rows(b % 4, new_span)], lsem.at[9 + y])

    @pl.when(core == 1)
    def _():
        for a in range(1, 5):
            own_remote(a).start()

    @pl.when(core == 0)
    def _():
        for a in range(1, 5):
            own_local(a).start()

    for y in range(2):
        j = y * 8 + 2 * (b // 4)

        @pl.when(j != b)
        def _():
            q_remote(y).start()

        @pl.when(j == b)
        def _():
            q_local(y).start()

    columns = lax.broadcasted_iota(jnp.int32, (1, bias.shape[1]), 1)
    bias[...] = jnp.where(columns < len_ref[0], 0.0, masked_score)

    for c in locals_:
        c.wait()

    def landed(a):
        for k in range(1, n_blk):
            pltpu.make_async_remote_copy(
                src_ref=srcs[a].at[:, lane(b)], dst_ref=mains[a].at[rows(b, srcs[a].shape[0])],
                send_sem=ss.at[a, k], recv_sem=rs.at[a, k], device_id=dev(b), device_id_type=MESH).wait_recv()

    for a in range(3):
        landed(a)

    lane_index = lax.broadcasted_iota(jnp.int32, (TILE, LANES), 1)
    low_half = lane_index < 64

    cached_chunks = 4

    def score(t, q, p0, keys_c, keys_n, new_chunks):
        row0 = t * TILE
        qt = q[pl.ds(pl.multiple_of(row0, TILE), TILE), :].astype(jnp.float32) * score_scale
        zero = jnp.zeros_like(qt)
        stacked = jnp.concatenate(
            [jnp.where(low_half, qt, zero), jnp.where(low_half, zero, qt)], axis=0).astype(jnp.bfloat16)
        best = None
        for c in range(cached_chunks + new_chunks):
            is_new = c >= cached_chunks
            keys = keys_n if is_new else keys_c
            k0 = (c - cached_chunks if is_new else c) * CHUNK
            s = lax.dot_general(
                stacked, keys[k0:k0 + CHUNK, :], (((1,), (1,)), ((), ())), preferred_element_type=jnp.float32)
            if is_new:
                at = lax.broadcasted_iota(jnp.int32, s.shape, 1) + k0
                pos = lax.broadcasted_iota(jnp.int32, s.shape, 0) % TILE + p0
                s = jnp.where(at <= pos, s, masked_score)
            else:
                s = s + bias[:, k0:k0 + CHUNK]
            sc[t, :, c * CHUNK:(c + 1) * CHUNK] = s
            for g in range(CHUNK // LANES):
                part = s[:, g * LANES:(g + 1) * LANES]
                best = part if best is None else jnp.maximum(best, part)
        tops[t] = jnp.max(best, axis=1, keepdims=True)

    def mix(t, vals_c, vals_n, new_chunks, out):
        row0 = t * TILE
        top = tops[t]
        total = None
        mixed = None
        for c in range(cached_chunks + new_chunks):
            is_new = c >= cached_chunks
            vals = vals_n if is_new else vals_c
            k0 = (c - cached_chunks if is_new else c) * CHUNK
            w = jnp.exp(sc[t, :, c * CHUNK:(c + 1) * CHUNK] - top)
            for g in range(CHUNK // LANES):
                part = w[:, g * LANES:(g + 1) * LANES]
                total = part if total is None else total + part
            o = jnp.dot(w.astype(jnp.bfloat16), vals[k0:k0 + CHUNK, :], preferred_element_type=jnp.float32)
            mixed = o if mixed is None else mixed + o
        mixed = mixed / jnp.sum(total, axis=1, keepdims=True)
        out[pl.ds(pl.multiple_of(row0, TILE), TILE), :] = jnp.where(
            low_half, mixed[:TILE], mixed[TILE:]).astype(jnp.bfloat16)

    @pl.loop(0, 4)
    def _(t):
        score(t, qb, t * TILE, kc, kn, 1)

    @pl.loop(4, 8)
    def _(t):
        score(t, qb, t * TILE, kc, kn, 2)

    for a in range(3, 5):
        landed(a)

    @pl.loop(0, 4)
    def _(t):
        mix(t, vc, vn, 1, ob)

    @pl.loop(4, 8)
    def _(t):
        mix(t, vc, vn, 2, ob)

    def back(k):
        j = (b + k) % n_blk
        return pltpu.make_async_remote_copy(
            src_ref=ob.at[rows(j, new_span)], dst_ref=att.at[:, lane(b)],
            send_sem=sso.at[k], recv_sem=rso.at[k], device_id=dev(j), device_id_type=MESH)

    backs = [back(k) for k in range(1, n_blk)]
    for c in backs:
        c.start()
    home = pltpu.make_async_copy(ob.at[rows(b, new_span)], att.at[:, lane(b)], lsem.at[11])
    home.start()

    def eback(i):
        return pltpu.make_async_remote_copy(
            src_ref=oe.at[rows(i, new_span)], dst_ref=att.at[:, lane(16 + half)],
            send_sem=ssoe.at[i], recv_sem=rsoe.at[half], device_id=dev(4 * quarter + i), device_id_type=MESH)

    def eback_local(i):
        return pltpu.make_async_copy(oe.at[rows(i, new_span)], att.at[:, lane(16 + half)], lsem.at[12])

    @pl.when(core == 0)
    def _():
        for a in range(1, 5):
            own_local(a).wait()
        for y in range(2):
            @pl.when(y * 8 + 2 * (b // 4) == b)
            def _():
                q_local(y).wait()
        for i in range(4):
            @pl.when((4 * quarter + i) != b)
            def _():
                pltpu.make_async_remote_copy(
                    src_ref=q_ref.at[:, lane(16)], dst_ref=qe.at[rows(i, new_span)],
                    send_sem=ssq.at[0], recv_sem=rsq.at[i], device_id=dev(b), device_id_type=MESH).wait_recv()
        for k in range(1, n_blk):
            s = (b + k) % n_blk
            for a in range(1, 5):
                pltpu.make_async_remote_copy(
                    src_ref=srcs[a].at[:, lane(16)], dst_ref=extras[a].at[rows(s, srcs[a].shape[0])],
                    send_sem=sse.at[a - 1, 0], recv_sem=rse.at[a - 1, s], device_id=dev(b),
                    device_id_type=MESH).wait_recv()

        @pl.loop(0, 2)
        def _(t):
            score(t, qe, quarter * 256 + t * TILE, kce, kne, 2)
            mix(t, vce, vne, 2, oe)

        for i in range(4):
            @pl.when((4 * quarter + i) != b)
            def _():
                eback(i).start()

            @pl.when((4 * quarter + i) == b)
            def _():
                eback_local(i).start()

    home.wait()
    for k in range(1, n_blk):
        pltpu.make_async_remote_copy(
            src_ref=ob.at[rows(b, new_span)], dst_ref=att.at[:, lane(b)],
            send_sem=sso.at[k], recv_sem=rso.at[k], device_id=dev(b), device_id_type=MESH).wait_recv()
    for y in range(2):
        j = y * 8 + 2 * (b // 4)

        @pl.when(j != b)
        def _():
            pltpu.make_async_remote_copy(
                src_ref=oe.at[rows(0, new_span)], dst_ref=att.at[:, lane(16 + y)],
                send_sem=ssoe.at[0], recv_sem=rsoe.at[y], device_id=dev(b), device_id_type=MESH).wait_recv()

        @pl.when(j == b)
        def _():
            pltpu.make_async_copy(oe.at[rows(0, new_span)], att.at[:, lane(16 + y)], lsem.at[12]).wait()

    wcopy.wait()
    width = 768
    squares = jnp.zeros((new_span, 1), jnp.float32)
    for c in range(q_ref.shape[1] // width):
        cols = slice(c * width, (c + 1) * width)
        h = (res_ref[:, cols].astype(jnp.float32)
             + jnp.dot(att[...], wv[:, cols], preferred_element_type=jnp.float32)).astype(jnp.bfloat16)
        hid_ref[:, cols] = h
        wide = h.astype(jnp.float32)
        squares = squares + jnp.sum(wide * wide, axis=1, keepdims=True)
    factor = lax.rsqrt(squares / q_ref.shape[1] + epsilon)
    norm_ref[...] = (hid_ref[...].astype(jnp.float32) * factor * gain_ref[...].reshape(1, q_ref.shape[1])).astype(jnp.bfloat16)

    for c in sends + esends + backs:
        c.wait_send()

    @pl.when(core == 1)
    def _():
        for a in range(1, 5):
            own_remote(a).wait_send()

    @pl.when(core == 0)
    def _():
        for i in range(4):
            @pl.when((4 * quarter + i) != b)
            def _():
                eback(i).wait_send()

    for y in range(2):
        @pl.when(y * 8 + 2 * (b // 4) != b)
        def _():
            q_remote(y).wait_send()


def attend(q, kn, vn, ck, cv, length, residual, gain, w_out):
    span, width = q.shape
    cache = ck.shape[0]
    bf = jnp.bfloat16
    dma = pltpu.SemaphoreType.DMA
    vmem = pl.BlockSpec(memory_space=pltpu.VMEM)
    hbm = pl.BlockSpec(memory_space=pl.ANY)
    v = lambda *s: pltpu.VMEM(s, bf)
    return pl.pallas_call(
        attend_kernel,
        out_shape=[jax.ShapeDtypeStruct((span, width), bf)] * 2,
        in_specs=[hbm] * 5 + [pl.BlockSpec(memory_space=pltpu.SMEM), hbm, vmem, hbm],
        out_specs=[vmem] * 2,
        scratch_shapes=[
            v(span, width), v(span, width), v(span, width), v(cache, width), v(cache, width), v(span, width), dma((6,)),
            v(16 * span, LANES), v(16 * cache, LANES), v(16 * span, LANES), v(16 * cache, LANES), v(16 * span, LANES),
            v(4 * span, LANES), v(16 * cache, LANES), v(16 * span, LANES), v(16 * cache, LANES), v(16 * span, LANES),
            pltpu.VMEM((8, 2 * TILE, 16 * (span + cache)), jnp.float32), pltpu.VMEM((8, 2 * TILE, 1), jnp.float32), pltpu.VMEM((1, 16 * cache), jnp.float32),
            v(16 * span, LANES), v(4 * span, LANES), v(span, width), v(width, width),
            dma((5, 16)), dma((5, 16)), dma((4, 8)), dma((4, 16)), dma((2,)), dma((4,)), dma((13,)),
            dma((16,)), dma((16,)), dma((4,)), dma((2,)), dma,
        ],
        compiler_params=pltpu.CompilerParams(collective_id=0, has_side_effects=True, vmem_limit_bytes=62 * 2**20),
        name="attend",
    )(q, kn, vn, ck, cv, length, residual, gain, w_out)


IN_WIDTHS = (768, 768, 768)
OUT_WIDTHS = (768, 768, 512, 256)
HEAD_ROWS = 72


def columns_of(widths, f):
    return slice(sum(widths[:f]), sum(widths[:f + 1]))


def expert_kernel(
    norm_ref, hid_ref, ids_hbm, gw_hbm, wg_hbm, wu_hbm, wd_hbm,
    out_ref,
    tok, slab, wg, wu, part, sibr, ring, term, ering, wd, weighted,
    cross, pick, gacc, uacc, act, ids_ref, gw_ref, slots, gates,
    ess, ers, bss, brs, fss, frs, pss, prs, rss, rrs, xss, xrs, lsem, wsem,
):
    b = lax.axis_index("blk")
    e = lax.axis_index("expert")
    h, x, core = b // 8, (b // 2) % 4, b % 2
    eh, ez = e // 4, e % 4
    span = norm_ref.shape[0]
    pieces = len(IN_WIDTHS)
    requests = tok[0].shape[0]
    in_across_first = (True, False, True)
    out_across_last = (True, False, True, True)

    def blk_dev(hh, xx, cc):
        return {"blk": hh * 8 + xx * 2 + cc}

    def exp_dev(hh, zz):
        return {"expert": hh * 4 + zz}

    b_right, b_left = blk_dev(h, (x + 1) % 4, core), blk_dev(h, (x + 3) % 4, core)
    b_across, b_sibling = blk_dev(1 - h, x, core), blk_dev(h, x, 1 - core)
    e_right, e_left, e_across = exp_dev(eh, (ez + 1) % 4), exp_dev(eh, (ez + 3) % 4), exp_dev(1 - eh, ez)

    bar = pltpu.get_barrier_semaphore()
    peers = (b_right, b_left, b_across, b_sibling, e_right, e_left, e_across)
    for peer in peers:
        pl.semaphore_signal(bar, inc=1, device_id=peer, device_id_type=MESH)
    small = [pltpu.make_async_copy(ids_hbm, ids_ref, lsem.at[pieces]), pltpu.make_async_copy(gw_hbm, gw_ref, lsem.at[pieces + 1])]
    for c in small:
        c.start()
    owns = []
    for f in range(pieces):
        owns.append(pltpu.make_async_copy(norm_ref.at[:, columns_of(IN_WIDTHS, f)], tok[f].at[e], lsem.at[f]))
        owns[-1].start()
    wcopies = []
    for i, (src, dst, widths) in enumerate(
            ((wg_hbm, wg, IN_WIDTHS), (wu_hbm, wu, IN_WIDTHS), (wd_hbm, wd, OUT_WIDTHS))):
        for f in range(len(widths)):
            wcopies.append(pltpu.make_async_copy(src.at[:, columns_of(widths, f)], dst[f], wsem.at[f, i]))
            wcopies[-1].start()
    pl.semaphore_wait(bar, len(peers))

    sent = []

    def remote(src, dst, ssem, rsem, device):
        return pltpu.make_async_remote_copy(
            src_ref=src, dst_ref=dst, send_sem=ssem, recv_sem=rsem, device_id=device, device_id_type=MESH)

    def send(src, dst, ssem, rsem, device):
        c = remote(src, dst, ssem, rsem, device)
        c.start()
        sent.append(c)

    def arrived(dst, ssem, rsem):
        remote(dst, dst, ssem, rsem, b_across).wait_recv()

    mid = span // 2
    low, high = pl.ds(0, mid), pl.ds(mid, mid)

    def eb(flip, off):
        return ((eh + flip) % 2) * 4 + (ez + off) % 4

    def eview(f, block, rows=None):
        return tok[f].at[block] if rows is None else tok[f].at[block, rows]

    def epost(f, i, block, device, rows=None):
        view = eview(f, block, rows)
        remote(view, view, ess.at[f, i], ers.at[f, i], device).start()

    def egot(f, i, block, rows=None):
        arrived(eview(f, block, rows), ess.at[f, i], ers.at[f, i])

    def expert_open(f):
        src = norm_ref.at[:, columns_of(IN_WIDTHS, f)]
        for i, device in enumerate((e_across, e_right, e_left)):
            remote(src, tok[f].at[e], ess.at[f, i], ers.at[f, i], device).start()

    def expert_middle(f):
        egot(f, 0, eb(1, 0))
        epost(f, 3, eb(1, 0), e_right)
        epost(f, 4, eb(1, 0), e_left)
        egot(f, 1, eb(0, 3))
        epost(f, 5, eb(0, 3), e_right, low)
        egot(f, 2, eb(0, 1))
        epost(f, 6, eb(0, 1), e_left, high)

    def expert_close(f):
        egot(f, 3, eb(1, 3))
        epost(f, 7, eb(1, 3), e_right, low)
        egot(f, 4, eb(1, 1))
        epost(f, 8, eb(1, 1), e_left, high)
        egot(f, 5, eb(0, 2), low)
        egot(f, 6, eb(0, 2), high)
        egot(f, 7, eb(1, 2), low)
        egot(f, 8, eb(1, 2), high)

    home = h * 4 + x
    mine = pl.ds(pl.multiple_of(core * CAP, 8), CAP)
    other = pl.ds(pl.multiple_of((1 - core) * CAP, 8), CAP)

    def select(f):
        acc = None
        for r in range(requests):
            o = jnp.dot(pick[r], tok[f][r], preferred_element_type=jnp.float32)
            acc = o if acc is None else acc + o
        slab[f][home, mine, :] = acc.astype(jnp.bfloat16)

    head, tail = pl.ds(0, HEAD_ROWS), pl.ds(HEAD_ROWS, CAP - HEAD_ROWS)

    def bb(flip, off):
        return ((h + flip) % 2) * 4 + (x + off) % 4

    def view_of(buf, f, block, rows=None):
        if rows is None:
            return buf[f].at[block, mine]
        return buf[f].at[block, pl.ds(pl.multiple_of(core * CAP + rows.start, 8), rows.size)]

    def bpost(f, i, block, device, rows=None):
        view = view_of(slab, f, block, rows)
        remote(view, view, bss.at[f, i], brs.at[f, i], device).start()

    def bgot(f, i, block, rows=None):
        arrived(view_of(slab, f, block, rows), bss.at[f, i], brs.at[f, i])

    def share(f, k, block):
        view = view_of(slab, f, block)
        remote(view, view, fss.at[f, k], frs.at[f, k], b_sibling).start()

    def gather(f, stage):
        if stage == 0:
            bpost(f, 1, home, b_right)
            bpost(f, 2, home, b_left)
            bpost(f, 0, home, b_across)
            share(f, 0, home)
        elif stage == 1:
            bgot(f, 1, bb(0, 3))
            bpost(f, 5, bb(0, 3), b_right, head)
            if not in_across_first[f]:
                bpost(f, 3, bb(0, 3), b_across)
            share(f, 1, bb(0, 3))
            bgot(f, 2, bb(0, 1))
            bpost(f, 6, bb(0, 1), b_left, tail)
            if not in_across_first[f]:
                bpost(f, 4, bb(0, 1), b_across)
            share(f, 2, bb(0, 1))
            bgot(f, 0, bb(1, 0))
            if in_across_first[f]:
                bpost(f, 3, bb(1, 0), b_right)
                bpost(f, 4, bb(1, 0), b_left)
            share(f, 3, bb(1, 0))
        elif stage == 2:
            if not in_across_first[f]:
                bgot(f, 5, bb(0, 2), head)
                bgot(f, 6, bb(0, 2), tail)
                bpost(f, 7, bb(0, 2), b_across)
                share(f, 6, bb(0, 2))
            bgot(f, 3, bb(1, 3))
            if in_across_first[f]:
                bpost(f, 7, bb(1, 3), b_right, head)
            share(f, 4, bb(1, 3))
            bgot(f, 4, bb(1, 1))
            if in_across_first[f]:
                bpost(f, 8, bb(1, 1), b_left, tail)
            share(f, 5, bb(1, 1))
            if in_across_first[f]:
                bgot(f, 5, bb(0, 2), head)
                bgot(f, 6, bb(0, 2), tail)
                share(f, 6, bb(0, 2))
        else:
            if in_across_first[f]:
                bgot(f, 7, bb(1, 2), head)
                bgot(f, 8, bb(1, 2), tail)
            else:
                bgot(f, 7, bb(1, 2))
            share(f, 7, bb(1, 2))

    offsets = (0, 3, 1, 0, 3, 1, 2, 2)
    flips = (0, 0, 0, 1, 1, 1, 0, 1)
    offset_code = sum(o * 4**i for i, o in enumerate(offsets))
    flip_code = sum(o * 2**i for i, o in enumerate(flips))
    order = {(f, o): k for k, (f, o) in enumerate(zip(flips, offsets))}

    expert_open(0)

    for c in small:
        c.wait()
    ids0, ids1 = ids_ref[:, 0, :], ids_ref[:, 1, :]
    hit0, hit1 = ids0 == e, ids1 == e
    routed = jnp.where(hit0 | hit1, 1.0, 0.0).astype(jnp.float32)
    upto = (lax.broadcasted_iota(jnp.int32, (span, span), 0) <= lax.broadcasted_iota(jnp.int32, (span, span), 1))
    rank = jnp.dot(routed.astype(jnp.bfloat16), jnp.where(upto, 1.0, 0.0).astype(jnp.bfloat16),
                   preferred_element_type=jnp.float32)
    before = (lax.broadcasted_iota(jnp.int32, (requests, requests), 1) < lax.broadcasted_iota(jnp.int32, (requests, requests), 0))
    ahead = jnp.sum(jnp.dot(jnp.where(before, 1.0, 0.0).astype(jnp.bfloat16), routed.astype(jnp.bfloat16),
                            preferred_element_type=jnp.float32), axis=1, keepdims=True)
    slots[...] = jnp.where(routed > 0, rank + ahead - 1.0, -1.0).astype(jnp.int32)
    gates[...] = jnp.where(hit0, gw_ref[:, 0, :], 0.0) + jnp.where(hit1, gw_ref[:, 1, :], 0.0)
    for r in range(requests):
        at = lax.broadcasted_iota(jnp.int32, (CAP, span), 0)
        pick[r] = jnp.where(at == slots[r:r + 1, :], 1.0, 0.0).astype(jnp.bfloat16)

    one = core * 0 + 1

    def project(f, first, last):
        def step(k, powers):
            p4, p2 = powers
            block = ((h + (flip_code // p2) % 2) % 2) * 4 + (x + (offset_code // p4) % 4) % 4
            arrived(slab[f].at[block, other], fss.at[f, k], frs.at[f, k])
            a = slab[f][block]
            g = lax.dot_general(a, wg[f][...], (((1,), (1,)), ((), ())), preferred_element_type=jnp.float32)
            u = lax.dot_general(a, wu[f][...], (((1,), (1,)), ((), ())), preferred_element_type=jnp.float32)
            if f:
                g = gacc[block] + g
                u = uacc[block] + u
            if f < pieces - 1:
                gacc[block] = g
                uacc[block] = u
            else:
                act[block] = (g / (1.0 + jnp.exp(-g)) * u).astype(jnp.bfloat16)
            return p4 * 4, p2 * 2

        lax.fori_loop(first, last, step, (one * 4**first, one * 2**first))

    expert_middle(0)
    expert_open(1)
    expert_close(0)
    for c in owns:
        c.wait()
    select(0)
    gather(0, 0)
    expert_middle(1)
    expert_open(2)
    expert_close(1)
    select(1)
    gather(1, 0)
    gather(0, 1)
    expert_middle(2)
    expert_close(2)
    select(2)
    gather(2, 0)
    gather(0, 2)
    gather(1, 1)
    gather(0, 3)
    gather(1, 2)
    gather(2, 1)
    for c in wcopies:
        c.wait()
    project(0, 0, 8)
    gather(1, 3)
    gather(2, 2)
    project(1, 0, 8)
    project(2, 0, 7)
    gather(2, 3)
    project(2, 7, 8)

    def down(f):
        def step(i, powers):
            p4, p2 = powers
            k = 7 - i
            block = ((h + (flip_code // p2) % 2) % 2) * 4 + (x + (offset_code // p4) % 4) % 4
            part[f][block] = jnp.dot(act[block], wd[f][...], preferred_element_type=jnp.float32).astype(jnp.bfloat16)
            remote(part[f].at[block, other], sibr[f].at[block], pss.at[f, k], prs.at[f, k], b_sibling).start()
            return p4 // 4, p2 // 2

        lax.fori_loop(0, 8, step, (one * 4**7, one * 2**7))

    def wide(value):
        return value.astype(jnp.float32)

    def pair_sum(f, flip, off):
        block = bb(flip, off)
        k = order[flip, off]
        arrived(sibr[f].at[block], pss.at[f, k], prs.at[f, k])
        return block, wide(part[f][block, mine, :]) + wide(sibr[f][block])

    def keep(f, block, val):
        part[f][block, mine, :] = val.astype(jnp.bfloat16)

    def rsend(f, i, src, dst, device):
        send(src, dst, rss.at[f, i], rrs.at[f, i], device)

    def rgot(f, i, dst):
        arrived(dst, rss.at[f, i], rrs.at[f, i])

    FAR, NEAR_L, NEAR_R, ROW_S, ROW_R = 0, 2, 4, 6, 7

    def slot(f, i, rows=None):
        return ring[f].at[i] if rows is None else ring[f].at[i, rows]

    def ring_far(f, flip, block):
        rsend(f, flip * 4, view_of(part, f, block, head), slot(f, FAR + flip, head), b_right)
        rsend(f, flip * 4 + 1, view_of(part, f, block, tail), slot(f, FAR + flip, tail), b_left)

    def ring_near(f, flip, right, right_val, left, left_val):
        rgot(f, flip * 4, slot(f, FAR + flip, head))
        keep(f, right, jnp.concatenate(
            [right_val[:HEAD_ROWS] + wide(ring[f][FAR + flip, :HEAD_ROWS, :]), right_val[HEAD_ROWS:]], axis=0))
        rsend(f, flip * 4 + 2, view_of(part, f, right), slot(f, NEAR_L + flip), b_right)
        rgot(f, flip * 4 + 1, slot(f, FAR + flip, tail))
        keep(f, left, jnp.concatenate(
            [left_val[:HEAD_ROWS], left_val[HEAD_ROWS:] + wide(ring[f][FAR + flip, HEAD_ROWS:, :])], axis=0))
        rsend(f, flip * 4 + 3, view_of(part, f, left), slot(f, NEAR_R + flip), b_left)

    def ring_end(f, flip, val):
        rgot(f, flip * 4 + 2, slot(f, NEAR_L + flip))
        rgot(f, flip * 4 + 3, slot(f, NEAR_R + flip))
        return val + wide(ring[f][NEAR_L + flip]) + wide(ring[f][NEAR_R + flip])

    def weigh(f, val):
        gate = None
        for r in range(requests):
            g = jnp.sum(jnp.where(pick[r] > 0, gates[r:r + 1, :], 0.0), axis=1, keepdims=True)
            gate = g if gate is None else gate + g
        weighted[f][...] = (gate * wide(val.astype(jnp.bfloat16))).astype(jnp.bfloat16)

    def reduce_stage(f, stage):
        if out_across_last[f]:
            if stage == 0:
                for flip in (1, 0):
                    block, val = pair_sum(f, flip, 2)
                    keep(f, block, val)
                    ring_far(f, flip, block)
            elif stage == 1:
                for flip in (1, 0):
                    right, right_val = pair_sum(f, flip, 1)
                    left, left_val = pair_sum(f, flip, 3)
                    ring_near(f, flip, right, right_val, left, left_val)
            elif stage == 2:
                block, val = pair_sum(f, 1, 0)
                ring[f][ROW_S] = ring_end(f, 1, val).astype(jnp.bfloat16)
                rsend(f, 8, slot(f, ROW_S), slot(f, ROW_R), b_across)
            else:
                block, val = pair_sum(f, 0, 0)
                val = ring_end(f, 0, val)
                rgot(f, 8, slot(f, ROW_R))
                weigh(f, val + wide(ring[f][ROW_R]))
        else:
            if stage == 0:
                for off in (2, 3, 1, 0):
                    block, val = pair_sum(f, 1, off)
                    keep(f, block, val)
                    rsend(f, 4 + off if off else 8, view_of(part, f, block), cross.at[(x + off) % 4], b_across)
            elif stage == 1:
                block, val = pair_sum(f, 0, 2)
                rgot(f, 6, cross.at[(x + 2) % 4])
                keep(f, block, val + wide(cross[(x + 2) % 4]))
                ring_far(f, 0, block)
            elif stage == 2:
                left, left_val = pair_sum(f, 0, 3)
                rgot(f, 7, cross.at[(x + 3) % 4])
                right, right_val = pair_sum(f, 0, 1)
                rgot(f, 5, cross.at[(x + 1) % 4])
                ring_near(f, 0, right, right_val + wide(cross[(x + 1) % 4]), left, left_val + wide(cross[(x + 3) % 4]))
            else:
                block, val = pair_sum(f, 0, 0)
                rgot(f, 8, cross.at[x])
                weigh(f, ring_end(f, 0, val + wide(cross[x])))

    def xsend(f, i, src, dst, device):
        send(src, dst, xss.at[f, i], xrs.at[f, i], device)

    def xgot(f, i, dst):
        arrived(dst, xss.at[f, i], xrs.at[f, i])

    def eslot(f, i, rows=None):
        return ering[f].at[i] if rows is None else ering[f].at[i, rows]

    def spread(f, flip, off):
        block = eb(flip, off)
        return block, lax.dot_general(
            pick[block], weighted[f][...], (((0,), (0,)), ((), ())), preferred_element_type=jnp.float32)

    def return_stage(f, stage):
        if stage == 0:
            for flip in (1, 0):
                block, val = spread(f, flip, 2)
                term[f][block] = val.astype(jnp.bfloat16)
                xsend(f, flip * 4, term[f].at[block, low], eslot(f, FAR + flip, low), e_right)
                xsend(f, flip * 4 + 1, term[f].at[block, high], eslot(f, FAR + flip, high), e_left)
        elif stage == 1:
            for flip in (1, 0):
                block, val = spread(f, flip, 1)
                xgot(f, flip * 4, eslot(f, FAR + flip, low))
                term[f][block] = jnp.concatenate(
                    [val[:mid] + wide(ering[f][FAR + flip, :mid, :]), val[mid:]], axis=0).astype(jnp.bfloat16)
                xsend(f, flip * 4 + 2, term[f].at[block], eslot(f, NEAR_L + flip), e_right)
                block, val = spread(f, flip, 3)
                xgot(f, flip * 4 + 1, eslot(f, FAR + flip, high))
                term[f][block] = jnp.concatenate(
                    [val[:mid], val[mid:] + wide(ering[f][FAR + flip, mid:, :])], axis=0).astype(jnp.bfloat16)
                xsend(f, flip * 4 + 3, term[f].at[block], eslot(f, NEAR_R + flip), e_left)
        else:
            flip = 3 - stage
            block, val = spread(f, flip, 0)
            xgot(f, flip * 4 + 2, eslot(f, NEAR_L + flip))
            xgot(f, flip * 4 + 3, eslot(f, NEAR_R + flip))
            val = val + wide(ering[f][NEAR_L + flip]) + wide(ering[f][NEAR_R + flip])
            if flip:
                ering[f][ROW_S] = val.astype(jnp.bfloat16)
                xsend(f, 8, eslot(f, ROW_S), eslot(f, ROW_R), e_across)
            else:
                xgot(f, 8, eslot(f, ROW_R))
                cols = columns_of(OUT_WIDTHS, f)
                out_ref[:, cols] = (wide(hid_ref[:, cols]) + val + wide(ering[f][ROW_R])).astype(jnp.bfloat16)

    down(0)
    reduce_stage(0, 0)
    down(1)
    reduce_stage(1, 0)
    reduce_stage(0, 1)
    down(2)
    reduce_stage(2, 0)
    reduce_stage(1, 1)
    reduce_stage(0, 2)
    down(3)
    reduce_stage(3, 0)
    reduce_stage(2, 1)
    reduce_stage(1, 2)
    reduce_stage(0, 3)
    return_stage(0, 0)
    reduce_stage(3, 1)
    reduce_stage(2, 2)
    return_stage(0, 1)
    reduce_stage(1, 3)
    return_stage(1, 0)
    reduce_stage(3, 2)
    reduce_stage(2, 3)
    return_stage(2, 0)
    return_stage(0, 2)
    return_stage(1, 1)
    reduce_stage(3, 3)
    return_stage(3, 0)
    return_stage(2, 1)
    return_stage(0, 3)
    return_stage(1, 2)
    return_stage(3, 1)
    return_stage(2, 2)
    return_stage(1, 3)
    return_stage(3, 2)
    return_stage(2, 3)
    return_stage(3, 3)

    for c in sent:
        c.wait_send()

    def drained(view, sems):
        remote(view, view, sems, sems, b_across).wait_send()

    for f in range(pieces):
        for i in range(9):
            drained(eview(f, e, None if i < 5 else low), ess.at[f, i])
        for i in range(9 if in_across_first[f] else 8):
            full = i < 5 or (i == 7 and not in_across_first[f])
            drained(view_of(slab, f, home, None if full else head if i % 2 else tail), bss.at[f, i])
        for k in range(8):
            drained(view_of(slab, f, home), fss.at[f, k])
    for f in range(len(OUT_WIDTHS)):
        for k in range(8):
            drained(view_of(part, f, home), pss.at[f, k])


def mix_experts(normed, hidden, ids, gate_weights, w_gate, w_up, w_down):
    span, width = normed.shape
    units = w_gate.shape[0]
    requests = ids.shape[0]
    pieces = max(len(IN_WIDTHS), len(OUT_WIDTHS))
    bf = jnp.bfloat16
    dma = pltpu.SemaphoreType.DMA
    vmem = pl.BlockSpec(memory_space=pltpu.VMEM)
    hbm = pl.BlockSpec(memory_space=pl.ANY)
    v = lambda *s: pltpu.VMEM(s, bf)
    f32 = lambda *s: pltpu.VMEM(s, jnp.float32)
    return pl.pallas_call(
        expert_kernel,
        out_shape=jax.ShapeDtypeStruct((span, width), bf),
        in_specs=[vmem] * 2 + [hbm] * 5,
        out_specs=vmem,
        scratch_shapes=[
            [v(requests, span, w) for w in IN_WIDTHS], [v(8, 2 * CAP, w) for w in IN_WIDTHS],
            [v(units, w) for w in IN_WIDTHS], [v(units, w) for w in IN_WIDTHS],
            [v(8, 2 * CAP, w) for w in OUT_WIDTHS], [v(8, CAP, w) for w in OUT_WIDTHS],
            [v(8, CAP, w) for w in OUT_WIDTHS], [v(requests, span, w) for w in OUT_WIDTHS],
            [v(8, span, w) for w in OUT_WIDTHS], [v(units, w) for w in OUT_WIDTHS], [v(CAP, w) for w in OUT_WIDTHS],
            v(4, CAP, OUT_WIDTHS[1]), v(requests, CAP, span),
            f32(8, 2 * CAP, units), f32(8, 2 * CAP, units), v(8, 2 * CAP, units),
            pltpu.VMEM(ids.shape, jnp.int32), f32(*gate_weights.shape),
            pltpu.VMEM((requests, span), jnp.int32), f32(requests, span),
            dma((pieces, 9)), dma((pieces, 9)), dma((pieces, 9)), dma((pieces, 9)), dma((pieces, 8)), dma((pieces, 8)),
            dma((pieces, 8)), dma((pieces, 8)), dma((pieces, 9)), dma((pieces, 9)), dma((pieces, 9)), dma((pieces, 9)),
            dma((pieces + 2,)), dma((pieces, 3)),
        ],
        compiler_params=pltpu.CompilerParams(collective_id=1, has_side_effects=True, vmem_limit_bytes=62 * 2**20),
        name="mix_experts",
    )(normed, hidden, ids, gate_weights, w_gate, w_up, w_down)


def shards(
    q_new,
    k_new,
    v_new,
    cache_k,
    cache_v,
    cache_len,
    residual,
    w_out,
    norm_gain,
    expert_ids,
    gate_weights,
    w_gate,
    w_up,
    w_down,
):
    hidden_state, normed = attend(
        q_new[:, 0, :], k_new[:, 0, :], v_new[:, 0, :], cache_k[:, 0, :], cache_v[:, 0, :], cache_len,
        residual[:, 0, :], norm_gain, w_out)
    layer_out = mix_experts(
        normed, hidden_state, jnp.transpose(expert_ids, (1, 2, 0)), jnp.transpose(gate_weights, (1, 2, 0)),
        w_gate[0], w_up[0], w_down[0])
    return layer_out[:, None, :]


def solution(mesh):
    in_specs = (
        P("blk", "expert", None),
        P("blk", "expert", None),
        P("blk", "expert", None),
        P("blk", "expert", None),
        P("blk", "expert", None),
        P("expert"),
        P("blk", "expert", None),
        P(),
        P(),
        P("blk", None, None),
        P("blk", None, None),
        P("expert", "blk", None),
        P("expert", "blk", None),
        P("expert", "blk", None),
    )
    out_specs = P("blk", "expert", None)
    return jax.shard_map(shards, mesh=mesh, in_specs=in_specs, out_specs=out_specs, check_vma=False)
```
